256 devices in a mesh: strike: 64 (over y, z, core), dip: 4 (over x).
Axes of the slice: x: 4, y: 4, z: 8, core: 2. Of those that a mesh axis runs over, the one named last changes fastest.
Arguments:
- slip_rate: float32 [3, 4096, 1024], P(None, 'strike', 'dip'), may hold values from -6 to 6
- history: bfloat16 [4, 3, 2, 1024, 4096], P(None, None, None, ('strike', 'dip')), may hold values from -6 to 6
- lengths: int32 [1024, 4096], P(('strike', 'dip')), may hold values from 1 to 4, as said below
- prestress: float32 [2, 4096, 1024], P(None, 'strike', 'dip'), may hold values from -8 to 8
- normal_stress: float32 [4096, 1024], P('strike', 'dip'), may hold values from 8 to 16
- direct_effect: float32 [4096, 1024], P('strike', 'dip'), may hold values from 0.01 to 0.04
- state_log: float32 [4096, 1024], P('strike', 'dip'), may hold values from 1 to 5
Outputs:
- next_rates: float32 [3, 4096, 1024], P(None, 'strike', 'dip')
- next_state: float32 [4096, 1024], P('strike', 'dip')
The draws below stay inside these ranges and needn't reach their ends.
Inputs may be any that keep to these rules, and one draw needn't show every extreme that they name: `lengths`: how many of the newest slip-rate spectra enter each wavenumber's stress transfer.
All inputs are finite; a program needn't handle non-finite values.
Results may differ from the reference program's by a relative error of at most 0.0003.
Values sent between devices are 32-bit elements; how exact they have to be, the bound alone decides.
No kernel may reach another device: no remote copies, remote signals or barrier semaphores. Data moves between devices by JAX's collectives and lax.ppermute only.
A program may use at most 128 MiB of HBM per device.

```python
import math
import jax
import jax.numpy as jnp

NX = 4096
NZ = 1024
HIST = 4
NEWTON = 2


def draw_lengths(key, part):
    dip_modes = jnp.arange(NZ, dtype=jnp.int32)[:, None]
    strike_modes = jnp.arange(NX, dtype=jnp.int32)[None, :]
    dip_size = jnp.where(2 * dip_modes < NZ, dip_modes, NZ - dip_modes) * (NX // NZ)
    strike_size = jnp.where(2 * strike_modes < NX, strike_modes, NX - strike_modes)
    square = strike_size * strike_size + dip_size * dip_size
    radius = NX // 4 * (NX // 4)
    reach_count = jnp.ones((NZ, NX), jnp.int32)
    for multiple in range(1, HIST):
        reach_count = reach_count + (multiple * multiple * square <= radius).astype(jnp.int32)
    jitter = jax.random.randint(key, (NZ, NX), -1, 2, dtype=jnp.int32)
    drawn_lengths = jnp.clip(reach_count + jitter, 1, HIST)
    drawn_lengths = jnp.where(square == 0, HIST, drawn_lengths)
    farthest = (2 * strike_modes == NX) & (2 * dip_modes == NZ)
    return jnp.where(farthest, 1, drawn_lengths).astype(jnp.int32)


def steps_of(stream_key, shape, pieces, smallest, largest):
    factor_of = 1.0
    for position, blocks in pieces:
        heights = jax.random.uniform(jax.random.fold_in(jax.random.fold_in(stream_key, 6), position), (blocks,), jnp.float32, smallest / len(pieces), largest / len(pieces))
        factor_of = factor_of * jnp.repeat(jnp.exp(heights), shape[position] // blocks).reshape((-1,) + (1,) * (len(shape) - 1 - position))
    return factor_of


def bell_draw(key, shape, deviation, most, pieces=(), kind=jnp.bfloat16):
    factor_of = steps_of(key, shape, pieces, -0.22, 0.18) if pieces else 1.0
    values = jax.random.normal(key, shape, jnp.float32) * deviation * factor_of
    return jnp.minimum(jnp.maximum(values, -most), most).astype(kind)


def setup_inputs(seed: int = 0) -> dict:
    key_list = jax.random.split(jax.random.key(seed), 8)
    slip_rate = bell_draw(key_list[0], (3, NX, NZ), 1.0, 6.0, ((1, 64), (2, 4)), jnp.float32)
    history = bell_draw(key_list[1], (HIST, 3, 2, NZ, NX), 1.0, 6.0, ((3, 256),))
    lengths = draw_lengths(jax.random.fold_in(key_list[7], 71), 0)
    prestress = bell_draw(key_list[3], (2, NX, NZ), 2.0, 8.0, ((1, 64), (2, 4)), jnp.float32)
    normal_stress = jnp.clip(8.0 + 8.0 * jax.random.uniform(key_list[4], (NX, NZ), jnp.float32) ** steps_of(key_list[4], (NX, NZ), ((0, 64), (1, 4)), -0.2, 0.2), 8.0, 16.0)
    direct_effect = jnp.clip(jnp.exp(math.log(0.04) - 1.3862944 * jax.random.uniform(key_list[5], (NX, NZ), jnp.float32) ** steps_of(key_list[5], (NX, NZ), ((0, 64), (1, 4)), -0.2, 0.2)), 0.01, 0.04)
    state_log = jnp.clip(1.0 + 4.0 * jax.random.uniform(key_list[6], (NX, NZ), jnp.float32) ** steps_of(key_list[6], (NX, NZ), ((0, 64), (1, 4)), -0.2, 0.2), 1.0, 5.0)
    return dict(slip_rate=slip_rate, history=history, lengths=lengths, prestress=prestress, normal_stress=normal_stress, direct_effect=direct_effect, state_log=state_log)


time_step = 0.5
coupling = 0.5
decay_rate = 0.05
shear_speed = 0.6
opening_speed = 1.7
radiation = 0.5
healing = 1.0
slip_length = 2.0

def area_sine(ratio):
    return jnp.log(ratio + jnp.sqrt(ratio * ratio + 1.0))

def wave_geometry(dip_modes, strike_modes, dip_cells, strike_cells):
    signed_dip = jnp.where(2 * dip_modes < dip_cells, dip_modes, dip_modes - dip_cells)
    signed_strike = jnp.where(2 * strike_modes < strike_cells, strike_modes, strike_modes - strike_cells)
    wave_dip = signed_dip.astype(jnp.float32) * (2.0 * math.pi / dip_cells)
    wave_strike = signed_strike.astype(jnp.float32) * (2.0 * math.pi / strike_cells)
    modulus = jnp.sqrt(wave_strike * wave_strike + wave_dip * wave_dip)
    anchor = (signed_dip == 0) & (signed_strike == 0)
    safe_modulus = jnp.where(anchor, 1.0, modulus)
    unit_strike = jnp.where(anchor, 1.0, wave_strike / safe_modulus)
    unit_dip = jnp.where(anchor, 0.0, wave_dip / safe_modulus)
    return (modulus, unit_strike, unit_dip)

def delay_mixing(geometry, delay):
    modulus, unit_strike, unit_dip = geometry
    phase_arg = modulus * (time_step * (delay + 1.0))
    envelope = -coupling * time_step * modulus * jnp.exp(-decay_rate * phase_arg)
    mode_two = envelope * jnp.cos(phase_arg)
    mode_three = envelope * jnp.cos(shear_speed * phase_arg)
    mode_one = envelope * jnp.cos(opening_speed * phase_arg)
    mix_along = unit_strike * unit_strike * mode_two + unit_dip * unit_dip * mode_three
    mix_cross = unit_strike * unit_dip * (mode_two - mode_three)
    mix_across = unit_dip * unit_dip * mode_two + unit_strike * unit_strike * mode_three
    return (mix_along, mix_cross, mix_across, mode_one)

def delay_term(spectrum, mixing, active):
    mix_along, mix_cross, mix_across, mode_one = mixing
    force_strike = (mix_along * spectrum[0] + mix_cross * spectrum[1]) * active
    force_dip = (mix_cross * spectrum[0] + mix_across * spectrum[1]) * active
    force_open = mode_one * spectrum[2] * active
    return jnp.stack([force_strike, force_dip, force_open])

def friction_step(force_field, prestress, normal_stress, direct_effect, state_log):
    load_strike = prestress[0] + force_field[0]
    load_dip = prestress[1] + force_field[1]
    traction = jnp.sqrt(load_strike * load_strike + load_dip * load_dip)
    strength = direct_effect * normal_stress
    factor = 2.0 * radiation * jnp.exp(-state_log)
    estimate = jnp.minimum(traction / strength, area_sine(traction / factor))
    for repeat in range(NEWTON):
        residual = traction - strength * estimate - factor * jnp.sinh(estimate)
        estimate = estimate + residual / (strength + factor * jnp.cosh(estimate))
    slip_speed = (traction - strength * estimate) / radiation
    unit_scale = slip_speed / jnp.maximum(traction, 1.0)
    new_rates = jnp.stack([unit_scale * load_strike, unit_scale * load_dip, force_field[2] / radiation])
    new_state = state_log + time_step * (healing * jnp.exp(-state_log) - slip_speed / slip_length)
    return (new_rates, new_state)

def to_spectrum(space_field):
    complex_field = jnp.transpose(jnp.fft.fft2(space_field, norm='ortho'), (0, 2, 1))
    return jnp.stack([jnp.real(complex_field), jnp.imag(complex_field)], axis=1)

def to_field(spectrum):
    complex_field = jnp.transpose(spectrum[:, 0] + 1j * spectrum[:, 1], (0, 2, 1))
    return jnp.real(jnp.fft.ifft2(complex_field, norm='ortho'))

def transfer(recent, history, lengths, geometry):
    recent_count = len(recent)
    summed = jnp.zeros(recent[0].shape, jnp.float32)
    for offset in range(HIST):
        if offset < recent_count:
            source = recent[offset]
        else:
            source = history[offset - recent_count].astype(jnp.float32)
        active = (offset < lengths).astype(jnp.float32)
        summed = summed + delay_term(source, delay_mixing(geometry, float(offset)), active)
    return summed

def reference(slip_rate, history, lengths, prestress, normal_stress, direct_effect, state_log):
    dip_modes = jnp.arange(NZ, dtype=jnp.int32)[:, None]
    strike_modes = jnp.arange(NX, dtype=jnp.int32)[None, :]
    geometry = wave_geometry(dip_modes, strike_modes, NZ, NX)
    first_spec = to_spectrum(slip_rate)
    force_field = to_field(transfer([first_spec], history, lengths, geometry))
    next_rates, next_state = friction_step(force_field, prestress, normal_stress, direct_effect, state_log)
    second_spec = to_spectrum(next_rates)
    force_field = to_field(transfer([second_spec, first_spec], history, lengths, geometry))
    next_rates, next_state = friction_step(force_field, prestress, normal_stress, direct_effect, next_state)
    return (next_rates, next_state)
```

```python
import math

import jax
import jax.numpy as jnp
import numpy as np
from jax import lax
from jax.experimental import pallas as pl
from jax.experimental.pallas import tpu as pltpu
from jax.sharding import PartitionSpec as P

NX, NZ = 4096, 1024
DEV = 256
ROWS = NX // DEV
MODES = NZ // DEV
NEWTON = 2
BOTH = ("strike", "dip")
F32, BF16 = jnp.float32, jnp.bfloat16


def split(value):
    high = value.astype(BF16)
    low = (value - high.astype(F32)).astype(BF16)
    return high, low


def split_table(table):
    table = np.asarray(table, np.float64)
    high = table.astype(np.float32).astype(jnp.bfloat16)
    low = (table - high.astype(np.float64)).astype(np.float32).astype(jnp.bfloat16)
    return np.stack([high, low])


def dft_table():
    index = np.arange(DEV)
    angle = 2 * np.pi * (np.outer(index, index) % DEV) / DEV
    return split_table(np.concatenate([np.cos(angle), np.sin(angle)], 0))


def inner_table(sign):
    angle = 2 * np.pi * (np.outer(np.arange(ROWS), np.arange(ROWS)) % ROWS) / ROWS
    cos, sin = np.cos(angle) / math.sqrt(NX), sign * np.sin(angle) / math.sqrt(NX)
    table = np.zeros((2, ROWS, MODES, 2, MODES, ROWS))
    for m in range(MODES):
        table[0, :, m, 0, m, :] = cos
        table[0, :, m, 1, m, :] = -sin
        table[1, :, m, 0, m, :] = sin
        table[1, :, m, 1, m, :] = cos
    return table.reshape(128, 128)


def twist_table():
    angle = 2 * np.pi * np.outer(np.arange(ROWS), np.arange(DEV)) / NX
    return np.stack([np.cos(angle), np.sin(angle)]).astype(np.float32)


def turn_table():
    angle = 2 * np.pi * np.outer(np.arange(MODES), np.arange(DEV)) / NZ
    table = np.stack([np.cos(angle), np.sin(angle)]) / math.sqrt(NZ)
    return table.reshape(2 * MODES, DEV).astype(np.float32)


def dot3(left, right):
    lh, ll = left
    rh, rl = right
    out = jnp.dot(lh, rh, preferred_element_type=F32)
    out += jnp.dot(ll, rh, preferred_element_type=F32)
    out += jnp.dot(lh, rl, preferred_element_type=F32)
    return out


def long_dft(blocks, dft, sign):
    rows = []
    for real, imag in blocks:
        if sign < 0:
            rows.append(jnp.concatenate([real, imag], 1))
            rows.append(jnp.concatenate([imag, -real], 1))
        else:
            rows.append(jnp.concatenate([real, -imag], 1))
            rows.append(jnp.concatenate([imag, real], 1))
    out = dot3(split(jnp.concatenate(rows, 0)), (dft[0], dft[1]))
    return [(out[128 * c : 128 * c + 64], out[128 * c + 64 : 128 * c + 128]) for c in range(3)]


def read_lines(ref):
    blocks = []
    for c in range(3):
        lines = ref[pl.ds(c, DEV, stride=3), :].T
        blocks.append((lines[:64], lines[64:]))
    return blocks


def write_lines(ref, blocks):
    for c, (real, imag) in enumerate(blocks):
        ref[pl.ds(c, DEV, stride=3), :] = jnp.concatenate([real, imag], 0).T


def dip_forward(field, turn):
    cos = [turn[m : m + 1, :] for m in range(4)]
    sin = [turn[4 + m : 5 + m, :] for m in range(4)]
    blocks = []
    for x0, x1, x2, x3 in field:
        even, odd, f, g = x0 + x2, x1 + x3, x0 - x2, x1 - x3
        y0, y2 = even + odd, even - odd
        real = [y0 * cos[0], f * cos[1] - g * sin[1], y2 * cos[2], f * cos[3] + g * sin[3]]
        imag = [
            jnp.zeros_like(y0),
            -(f * sin[1] + g * cos[1]),
            -(y2 * sin[2]),
            g * cos[3] - f * sin[3],
        ]
        blocks.append((jnp.concatenate(real, 0), jnp.concatenate(imag, 0)))
    return blocks


def dip_inverse(blocks, turn):
    cos = [turn[m : m + 1, :] for m in range(4)]
    sin = [turn[4 + m : 5 + m, :] for m in range(4)]
    field = []
    for real, imag in blocks:
        re = [real[16 * m : 16 * m + 16] for m in range(4)]
        im = [imag[16 * m : 16 * m + 16] for m in range(4)]
        u = [cos[m] * re[m] - sin[m] * im[m] for m in range(4)]
        v1 = cos[1] * im[1] + sin[1] * re[1]
        v3 = cos[3] * im[3] + sin[3] * re[3]
        a, b, c, d = u[0] + u[2], u[0] - u[2], u[1] + u[3], v3 - v1
        field.append([a + c, b + d, a - c, b - d])
    return field


def friction(force, prestress, strength, state):
    load_strike = prestress[0] + force[0]
    load_dip = prestress[1] + force[1]
    traction = jnp.sqrt(load_strike * load_strike + load_dip * load_dip)
    factor = jnp.exp(-state)
    ratio = traction / factor
    estimate = jnp.minimum(traction / strength, jnp.log(ratio + jnp.sqrt(ratio * ratio + 1.0)))
    for _ in range(NEWTON):
        up, down = jnp.exp(estimate), jnp.exp(-estimate)
        half = 0.5 * factor
        residual = traction - strength * estimate - half * (up - down)
        estimate = estimate + residual / (strength + half * (up + down))
    slip_speed = 2.0 * (traction - strength * estimate)
    scale = slip_speed / jnp.maximum(traction, 1.0)
    rates = [scale * load_strike, scale * load_dip, 2.0 * force[2]]
    return rates, state + 0.5 * (factor - 0.5 * slip_speed)


def pack_kernel(slip, prestress, normal, effect, state, out):
    for d in range(4):
        rows = slice(16 * d, 16 * d + 16)
        for c in range(3):
            out[d, 16 * c : 16 * c + 16, :] = slip[c, rows, :]
        for c in range(2):
            out[d, 48 + 16 * c : 64 + 16 * c, :] = prestress[c, rows, :]
        out[d, 80:96, :] = normal[rows, :] * effect[rows, :]
        out[d, 96:112, :] = state[rows, :]


def first_kernel(fields, turn, dft, out):
    field = [[fields[d, 16 * c : 16 * c + 16, :] for d in range(4)] for c in range(3)]
    write_lines(out, long_dft(dip_forward(field, turn), dft, -1))


def space_step(lines, fields, state, turn, dft):
    field = dip_inverse(long_dft(read_lines(lines), dft, 1), turn)
    force = [jnp.concatenate(f, 0) for f in field]

    def quarter(at):
        return jnp.concatenate([fields[d, at : at + 16, :] for d in range(4)], 0)

    return friction(force, (quarter(48), quarter(64)), quarter(80), state(quarter))


def middle_kernel(lines, fields, turn, dft, out, state_out):
    rates, state = space_step(lines, fields, lambda quarter: quarter(96), turn, dft)
    state_out[...] = state
    field = [[r[16 * d : 16 * d + 16] for d in range(4)] for r in rates]
    write_lines(out, long_dft(dip_forward(field, turn), dft, -1))


def last_kernel(lines, fields, state_in, turn, dft, out):
    rates, state = space_step(lines, fields, lambda quarter: state_in[...], turn, dft)
    for d in range(4):
        for c, value in enumerate(rates + [state]):
            out[d, 16 * c : 16 * c + 16, :] = value[16 * d : 16 * d + 16]


def unpack_kernel(gathered, rates, state):
    for d in range(4):
        rows = slice(16 * d, 16 * d + 16)
        for c in range(3):
            rates[c, rows, :] = gathered[d, 16 * c : 16 * c + 16, :]
        state[rows, :] = gathered[d, 48:64, :]


def mixing(device):
    shape = (64, DEV)
    row = lax.broadcasted_iota(jnp.int32, shape, 0)
    kx = (row >> 2) * DEV + lax.broadcasted_iota(jnp.int32, shape, 1)
    kz = device * MODES + (row & 3)
    mz = jnp.where(2 * kz < NZ, kz, kz - NZ)
    mx = jnp.where(2 * kx < NX, kx, kx - NX)
    qz = mz.astype(F32) * (2.0 * math.pi / NZ)
    qx = mx.astype(F32) * (2.0 * math.pi / NX)
    q = jnp.sqrt(qx * qx + qz * qz)
    anchor = (mz == 0) & (mx == 0)
    safe = jnp.where(anchor, 1.0, q)
    ex = jnp.where(anchor, 1.0, qx / safe)
    ez = jnp.where(anchor, 0.0, qz / safe)
    xx, xz, zz = ex * ex, ex * ez, ez * ez
    decay = jnp.exp(-0.025 * q)
    envelope = -0.25 * q
    first = [jnp.cos(0.5 * s * q) for s in (1.0, 0.6, 1.7)]
    before = [jnp.ones(shape, F32)] * 3
    now = first
    out = []
    for lag in range(4):
        envelope = envelope * decay
        two, three, one = [envelope * c for c in now]
        out.append((xx * two + zz * three, xz * (two - three), zz * two + xx * three, one))
        now, before = [2.0 * f * c - p for f, c, p in zip(first, now, before)], now
    return out


def history_kernel(history, lengths, past1, past2, coef, held, reach):
    device = lax.axis_index("strike") * 4 + lax.axis_index("dip")
    for k1 in range(16):
        lanes = slice(DEV * k1, DEV * k1 + DEV)
        rows = slice(4 * k1, 4 * k1 + 4)
        reach[rows, :] = lengths[:, lanes].astype(F32)
    for lag in range(3):
        for c in range(3):
            for part in range(2):
                line = history[lag, c, part].astype(F32)
                for k1 in range(16):
                    held[lag, c, part, 4 * k1 : 4 * k1 + 4, :] = line[:, DEV * k1 : DEV * k1 + DEV]
    mix = mixing(device)
    length = reach[...]
    masked = [None] + [
        [jnp.where(length > float(lag), m, 0.0) for m in mix[lag]] for lag in range(1, 4)
    ]
    for i in range(4):
        coef[i] = mix[0][i]
        coef[4 + i] = masked[1][i]
    for out, skip in ((past1, 1), (past2, 2)):
        for part in range(2):
            total = [0.0, 0.0, 0.0]
            for lag in range(skip, 4):
                ss, sd, dd, op = masked[lag]
                a, b, c = [held[lag - skip, i, part] for i in range(3)]
                total[0] = total[0] + (ss * a + sd * b)
                total[1] = total[1] + (sd * a + dd * b)
                total[2] = total[2] + op * c
            for i in range(3):
                out[i, 64 * part : 64 * part + 64, :] = total[i]


def spectrum_of(lines, twist, dft, inner):
    blocks = long_dft(read_lines(lines), dft, -1)
    cos = jnp.concatenate([twist[0]] * 4, 0)
    sin = jnp.concatenate([twist[1]] * 4, 0)
    turned = [
        jnp.concatenate([re * cos + im * sin, im * cos - re * sin], 0) for re, im in blocks
    ]
    return dot3((inner[0], inner[1]), split(jnp.concatenate(turned, 1)))


def lines_of(out, force, twist, dft, inner):
    blocks = dot3((inner[0], inner[1]), split(jnp.concatenate(force, 1)))
    cos = jnp.concatenate([twist[0]] * 4, 0)
    sin = jnp.concatenate([twist[1]] * 4, 0)
    turned = []
    for c in range(3):
        re, im = blocks[:64, DEV * c : DEV * c + DEV], blocks[64:, DEV * c : DEV * c + DEV]
        turned.append((re * cos - im * sin, im * cos + re * sin))
    write_lines(out, long_dft(turned, dft, 1))


def apply_mix(coef, at, spec):
    both = [jnp.concatenate([coef[at + i]] * 2, 0) for i in range(4)]
    s, d, o = [spec[:, DEV * c : DEV * c + DEV] for c in range(3)]
    return [both[0] * s + both[1] * d, both[1] * s + both[2] * d, both[3] * o]


def mode_kernel_first(lines, past, coef, twist, dft, inner, back, out, spec_out):
    spec = spectrum_of(lines, twist, dft, inner)
    spec_out[...] = spec
    force = [f + past[c] for c, f in enumerate(apply_mix(coef, 0, spec))]
    lines_of(out, force, twist, dft, back)


def mode_kernel_second(lines, past, coef, older, twist, dft, inner, back, out):
    spec = spectrum_of(lines, twist, dft, inner)
    new, old = apply_mix(coef, 0, spec), apply_mix(coef, 4, older)
    force = [new[c] + old[c] + past[c] for c in range(3)]
    lines_of(out, force, twist, dft, back)


def call(kernel, outs, *args, scratch=()):
    return pl.pallas_call(
        kernel,
        out_shape=[jax.ShapeDtypeStruct(s, F32) for s in outs],
        scratch_shapes=scratch,
    )(*args)


def exchange(lines):
    return lax.all_to_all(lines.reshape(DEV, 1, 384), BOTH, 0, 0, tiled=True).reshape(768, 128)


def shards(slip_rate, history, lengths, prestress, normal_stress, direct_effect, state_log):
    dft = dft_table()
    inner = split_table(inner_table(-1.0))
    back = split_table(inverse_inner())
    twist, turn = twist_table(), turn_table()
    lines = (768, 128)

    (packed,) = call(
        pack_kernel, [(4, 112, 256)], slip_rate, prestress, normal_stress, direct_effect, state_log
    )
    fields = lax.all_to_all(packed, "dip", 0, 0, tiled=True)
    past1, past2, coef = call(
        history_kernel,
        [(3, 128, 256), (3, 128, 256), (8, 64, 256)],
        history,
        lengths,
        scratch=[pltpu.VMEM((3, 3, 2, 64, 256), F32), pltpu.VMEM((64, 256), F32)],
    )
    (out,) = call(first_kernel, [lines], fields, turn, dft)
    out, spec = call(
        mode_kernel_first, [lines, (128, 768)], exchange(out), past1, coef, twist, dft, inner, back
    )
    out, state = call(
        middle_kernel, [lines, (64, 256)], exchange(out), fields, turn, dft
    )
    (out,) = call(
        mode_kernel_second, [lines], exchange(out), past2, coef, spec, twist, dft, inner, back
    )
    (out,) = call(last_kernel, [(4, 64, 256)], exchange(out), fields, state, turn, dft)
    gathered = lax.all_to_all(out, "dip", 0, 0, tiled=True)
    rates, state = call(unpack_kernel, [(3, 64, 256), (64, 256)], gathered)
    return rates, state


def inverse_inner():
    forward = inner_table(-1.0).reshape(2, ROWS, MODES, 2, MODES, ROWS)
    return forward.transpose(3, 4, 5, 0, 1, 2).reshape(128, 128)


def solution(mesh):
    return jax.shard_map(
        shards,
        mesh=mesh,
        in_specs=(
            P(None, "strike", "dip"),
            P(None, None, None, ("strike", "dip"), None),
            P(("strike", "dip"), None),
            P(None, "strike", "dip"),
            P("strike", "dip"),
            P("strike", "dip"),
            P("strike", "dip"),
        ),
        out_specs=(P(None, "strike", "dip"), P("strike", "dip")),
        check_vma=False,
    )
```

```python
import math

import jax
import jax.numpy as jnp
import numpy as np
from jax import lax
from jax.experimental import pallas as pl
from jax.experimental.pallas import tpu as pltpu
from jax.sharding import PartitionSpec as P

NX, NZ = 4096, 1024
DEV = 256
ROWS = NX // DEV
MODES = NZ // DEV
NEWTON = 2
BOTH = ("strike", "dip")
F32, BF16 = jnp.float32, jnp.bfloat16


def split(value):
    high = value.astype(BF16)
    low = (value - high.astype(F32)).astype(BF16)
    return high, low


def split_table(table):
    table = np.asarray(table, np.float64)
    high = table.astype(np.float32).astype(jnp.bfloat16)
    low = (table - high.astype(np.float64)).astype(np.float32).astype(jnp.bfloat16)
    return np.stack([high, low])


def dft_table():
    index = np.arange(DEV)
    angle = 2 * np.pi * (np.outer(index, index) % DEV) / DEV
    return split_table(np.concatenate([np.cos(angle), np.sin(angle)], 0))


def inner_table(sign):
    angle = 2 * np.pi * (np.outer(np.arange(ROWS), np.arange(ROWS)) % ROWS) / ROWS
    cos, sin = np.cos(angle) / math.sqrt(NX), sign * np.sin(angle) / math.sqrt(NX)
    table = np.zeros((2, ROWS, MODES, 2, MODES, ROWS))
    for m in range(MODES):
        table[0, :, m, 0, m, :] = cos
        table[0, :, m, 1, m, :] = -sin
        table[1, :, m, 0, m, :] = sin
        table[1, :, m, 1, m, :] = cos
    return table.reshape(128, 128)


def twist_table():
    angle = 2 * np.pi * np.outer(np.arange(ROWS), np.arange(DEV)) / NX
    return np.stack([np.cos(angle), np.sin(angle)]).astype(np.float32)


def turn_table():
    angle = 2 * np.pi * np.outer(np.arange(MODES), np.arange(DEV)) / NZ
    table = np.stack([np.cos(angle), np.sin(angle)]) / math.sqrt(NZ)
    return table.reshape(2 * MODES, DEV).astype(np.float32)


def dot3(left, right):
    lh, ll = left
    rh, rl = right
    out = jnp.dot(lh, rh, preferred_element_type=F32)
    out += jnp.dot(ll, rh, preferred_element_type=F32)
    out += jnp.dot(lh, rl, preferred_element_type=F32)
    return out


def long_dft(blocks, dft, sign):
    rows = []
    for real, imag in blocks:
        if sign < 0:
            rows.append(jnp.concatenate([real, imag], 1))
            rows.append(jnp.concatenate([imag, -real], 1))
        else:
            rows.append(jnp.concatenate([real, -imag], 1))
            rows.append(jnp.concatenate([imag, real], 1))
    out = dot3(split(jnp.concatenate(rows, 0)), (dft[0], dft[1]))
    return [(out[128 * c : 128 * c + 64], out[128 * c + 64 : 128 * c + 128]) for c in range(3)]


def read_lines(ref):
    blocks = []
    for c in range(3):
        lines = ref[pl.ds(c, DEV, stride=3), :].T
        blocks.append((lines[:64], lines[64:]))
    return blocks


def write_lines(ref, blocks):
    for c, (real, imag) in enumerate(blocks):
        ref[pl.ds(c, DEV, stride=3), :] = jnp.concatenate([real, imag], 0).T


def dip_forward(field, turn):
    cos = [turn[m : m + 1, :] for m in range(4)]
    sin = [turn[4 + m : 5 + m, :] for m in range(4)]
    blocks = []
    for x0, x1, x2, x3 in field:
        even, odd, f, g = x0 + x2, x1 + x3, x0 - x2, x1 - x3
        y0, y2 = even + odd, even - odd
        real = [y0 * cos[0], f * cos[1] - g * sin[1], y2 * cos[2], f * cos[3] + g * sin[3]]
        imag = [
            jnp.zeros_like(y0),
            -(f * sin[1] + g * cos[1]),
            -(y2 * sin[2]),
            g * cos[3] - f * sin[3],
        ]
        blocks.append((jnp.concatenate(real, 0), jnp.concatenate(imag, 0)))
    return blocks


def dip_inverse(blocks, turn):
    cos = [turn[m : m + 1, :] for m in range(4)]
    sin = [turn[4 + m : 5 + m, :] for m in range(4)]
    field = []
    for real, imag in blocks:
        re = [real[16 * m : 16 * m + 16] for m in range(4)]
        im = [imag[16 * m : 16 * m + 16] for m in range(4)]
        u = [cos[m] * re[m] - sin[m] * im[m] for m in range(4)]
        v1 = cos[1] * im[1] + sin[1] * re[1]
        v3 = cos[3] * im[3] + sin[3] * re[3]
        a, b, c, d = u[0] + u[2], u[0] - u[2], u[1] + u[3], v3 - v1
        field.append([a + c, b + d, a - c, b - d])
    return field


def friction(force, prestress, strength, state):
    load_strike = prestress[0] + force[0]
    load_dip = prestress[1] + force[1]
    traction = jnp.sqrt(load_strike * load_strike + load_dip * load_dip)
    factor = jnp.exp(-state)
    ratio = traction / factor
    estimate = jnp.minimum(traction / strength, jnp.log(ratio + jnp.sqrt(ratio * ratio + 1.0)))
    for _ in range(NEWTON):
        up, down = jnp.exp(estimate), jnp.exp(-estimate)
        half = 0.5 * factor
        residual = traction - strength * estimate - half * (up - down)
        estimate = estimate + residual / (strength + half * (up + down))
    slip_speed = 2.0 * (traction - strength * estimate)
    scale = slip_speed / jnp.maximum(traction, 1.0)
    rates = [scale * load_strike, scale * load_dip, 2.0 * force[2]]
    return rates, state + 0.5 * (factor - 0.5 * slip_speed)


def pack_kernel(slip, prestress, normal, effect, state, out):
    for d in range(4):
        rows = slice(16 * d, 16 * d + 16)
        for c in range(3):
            out[d, 16 * c : 16 * c + 16, :] = slip[c, rows, :]
        for c in range(2):
            out[d, 48 + 16 * c : 64 + 16 * c, :] = prestress[c, rows, :]
        out[d, 80:96, :] = normal[rows, :] * effect[rows, :]
        out[d, 96:112, :] = state[rows, :]


def first_kernel(fields, turn, dft, out):
    field = [[fields[d, 16 * c : 16 * c + 16, :] for d in range(4)] for c in range(3)]
    write_lines(out, long_dft(dip_forward(field, turn), dft, -1))


def space_step(lines, fields, state, turn, dft):
    field = dip_inverse(long_dft(read_lines(lines), dft, 1), turn)
    force = [jnp.concatenate(f, 0) for f in field]

    def quarter(at):
        return jnp.concatenate([fields[d, at : at + 16, :] for d in range(4)], 0)

    return friction(force, (quarter(48), quarter(64)), quarter(80), state(quarter))


def middle_kernel(lines, fields, turn, dft, out, state_out):
    rates, state = space_step(lines, fields, lambda quarter: quarter(96), turn, dft)
    state_out[...] = state
    field = [[r[16 * d : 16 * d + 16] for d in range(4)] for r in rates]
    write_lines(out, long_dft(dip_forward(field, turn), dft, -1))


def last_kernel(lines, fields, state_in, turn, dft, out):
    rates, state = space_step(lines, fields, lambda quarter: state_in[...], turn, dft)
    for d in range(4):
        for c, value in enumerate(rates + [state]):
            out[d, 16 * c : 16 * c + 16, :] = value[16 * d : 16 * d + 16]


def unpack_kernel(gathered, rates, state):
    for d in range(4):
        rows = slice(16 * d, 16 * d + 16)
        for c in range(3):
            rates[c, rows, :] = gathered[d, 16 * c : 16 * c + 16, :]
        state[rows, :] = gathered[d, 48:64, :]


def mixing(device):
    shape = (64, DEV)
    row = lax.broadcasted_iota(jnp.int32, shape, 0)
    kx = (row >> 2) * DEV + lax.broadcasted_iota(jnp.int32, shape, 1)
    kz = device * MODES + (row & 3)
    mz = jnp.where(2 * kz < NZ, kz, kz - NZ)
    mx = jnp.where(2 * kx < NX, kx, kx - NX)
    qz = mz.astype(F32) * (2.0 * math.pi / NZ)
    qx = mx.astype(F32) * (2.0 * math.pi / NX)
    q = jnp.sqrt(qx * qx + qz * qz)
    anchor = (mz == 0) & (mx == 0)
    safe = jnp.where(anchor, 1.0, q)
    ex = jnp.where(anchor, 1.0, qx / safe)
    ez = jnp.where(anchor, 0.0, qz / safe)
    xx, xz, zz = ex * ex, ex * ez, ez * ez
    decay = jnp.exp(-0.025 * q)
    envelope = -0.25 * q
    first = [jnp.cos(0.5 * s * q) for s in (1.0, 0.6, 1.7)]
    before = [jnp.ones(shape, F32)] * 3
    now = first
    out = []
    for lag in range(4):
        envelope = envelope * decay
        two, three, one = [envelope * c for c in now]
        out.append((xx * two + zz * three, xz * (two - three), zz * two + xx * three, one))
        now, before = [2.0 * f * c - p for f, c, p in zip(first, now, before)], now
    return out


def history_kernel(history, lengths, past1, past2, coef, held, reach):
    device = lax.axis_index("strike") * 4 + lax.axis_index("dip")
    for k1 in range(16):
        lanes = slice(DEV * k1, DEV * k1 + DEV)
        rows = slice(4 * k1, 4 * k1 + 4)
        reach[rows, :] = lengths[:, lanes].astype(F32)
    for lag in range(3):
        for c in range(3):
            for part in range(2):
                line = history[lag, c, part].astype(F32)
                for k1 in range(16):
                    held[lag, c, part, 4 * k1 : 4 * k1 + 4, :] = line[:, DEV * k1 : DEV * k1 + DEV]
    mix = mixing(device)
    length = reach[...]
    masked = [None] + [
        [jnp.where(length > float(lag), m, 0.0) for m in mix[lag]] for lag in range(1, 4)
    ]
    for i in range(4):
        coef[i] = mix[0][i]
        coef[4 + i] = masked[1][i]
    for out, skip in ((past1, 1), (past2, 2)):
        for part in range(2):
            total = [0.0, 0.0, 0.0]
            for lag in range(skip, 4):
                ss, sd, dd, op = masked[lag]
                a, b, c = [held[lag - skip, i, part] for i in range(3)]
                total[0] = total[0] + (ss * a + sd * b)
                total[1] = total[1] + (sd * a + dd * b)
                total[2] = total[2] + op * c
            for i in range(3):
                out[i, 64 * part : 64 * part + 64, :] = total[i]


def spectrum_of(lines, twist, dft, inner):
    blocks = long_dft(read_lines(lines), dft, -1)
    cos = jnp.concatenate([twist[0]] * 4, 0)
    sin = jnp.concatenate([twist[1]] * 4, 0)
    turned = [
        jnp.concatenate([re * cos + im * sin, im * cos - re * sin], 0) for re, im in blocks
    ]
    return dot3((inner[0], inner[1]), split(jnp.concatenate(turned, 1)))


def lines_of(out, force, twist, dft, inner):
    blocks = dot3((inner[0], inner[1]), split(jnp.concatenate(force, 1)))
    cos = jnp.concatenate([twist[0]] * 4, 0)
    sin = jnp.concatenate([twist[1]] * 4, 0)
    turned = []
    for c in range(3):
        re, im = blocks[:64, DEV * c : DEV * c + DEV], blocks[64:, DEV * c : DEV * c + DEV]
        turned.append((re * cos - im * sin, im * cos + re * sin))
    write_lines(out, long_dft(turned, dft, 1))


def apply_mix(coef, at, spec):
    both = [jnp.concatenate([coef[at + i]] * 2, 0) for i in range(4)]
    s, d, o = [spec[:, DEV * c : DEV * c + DEV] for c in range(3)]
    return [both[0] * s + both[1] * d, both[1] * s + both[2] * d, both[3] * o]


def mode_kernel_first(lines, past, coef, twist, dft, inner, back, out, spec_out):
    spec = spectrum_of(lines, twist, dft, inner)
    spec_out[...] = spec
    force = [f + past[c] for c, f in enumerate(apply_mix(coef, 0, spec))]
    lines_of(out, force, twist, dft, back)


def mode_kernel_second(lines, past, coef, older, twist, dft, inner, back, out):
    spec = spectrum_of(lines, twist, dft, inner)
    new, old = apply_mix(coef, 0, spec), apply_mix(coef, 4, older)
    force = [new[c] + old[c] + past[c] for c in range(3)]
    lines_of(out, force, twist, dft, back)


def call(kernel, outs, *args, scratch=(), grant=20):
    return pl.pallas_call(
        kernel,
        out_shape=[jax.ShapeDtypeStruct(s, F32) for s in outs],
        scratch_shapes=scratch,
        compiler_params=pltpu.CompilerParams(vmem_limit_bytes=grant << 20),
    )(*args)


def exchange(lines):
    return lax.all_to_all(lines.reshape(DEV, 1, 384), BOTH, 0, 0, tiled=True).reshape(768, 128)


def shards(slip_rate, history, lengths, prestress, normal_stress, direct_effect, state_log):
    dft = dft_table()
    inner = split_table(inner_table(-1.0))
    back = split_table(inverse_inner())
    twist, turn = twist_table(), turn_table()
    lines = (768, 128)

    (packed,) = call(
        pack_kernel,
        [(4, 112, 256)],
        slip_rate,
        prestress,
        normal_stress,
        direct_effect,
        state_log,
        grant=60,
    )
    fields = lax.all_to_all(packed, "dip", 0, 0, tiled=True)
    past1, past2, coef = call(
        history_kernel,
        [(3, 128, 256), (3, 128, 256), (8, 64, 256)],
        history,
        lengths,
        scratch=[pltpu.VMEM((3, 3, 2, 64, 256), F32), pltpu.VMEM((64, 256), F32)],
    )
    (out,) = call(first_kernel, [lines], fields, turn, dft)
    out, spec = call(
        mode_kernel_first, [lines, (128, 768)], exchange(out), past1, coef, twist, dft, inner, back
    )
    out, state = call(
        middle_kernel, [lines, (64, 256)], exchange(out), fields, turn, dft
    )
    (out,) = call(
        mode_kernel_second, [lines], exchange(out), past2, coef, spec, twist, dft, inner, back
    )
    (out,) = call(last_kernel, [(4, 64, 256)], exchange(out), fields, state, turn, dft)
    gathered = lax.all_to_all(out, "dip", 0, 0, tiled=True)
    rates, state = call(unpack_kernel, [(3, 64, 256), (64, 256)], gathered)
    return rates, state


def inverse_inner():
    forward = inner_table(-1.0).reshape(2, ROWS, MODES, 2, MODES, ROWS)
    return forward.transpose(3, 4, 5, 0, 1, 2).reshape(128, 128)


def solution(mesh):
    return jax.shard_map(
        shards,
        mesh=mesh,
        in_specs=(
            P(None, "strike", "dip"),
            P(None, None, None, ("strike", "dip"), None),
            P(("strike", "dip"), None),
            P(None, "strike", "dip"),
            P("strike", "dip"),
            P("strike", "dip"),
            P("strike", "dip"),
        ),
        out_specs=(P(None, "strike", "dip"), P("strike", "dip")),
        check_vma=False,
    )
```

```python
import math

import jax
import jax.numpy as jnp
import numpy as np
from jax import lax
from jax.experimental import pallas as pl
from jax.experimental.pallas import tpu as pltpu
from jax.sharding import PartitionSpec as P

NX, NZ = 4096, 1024
DEV = 256
ROWS = NX // DEV
MODES = NZ // DEV
NEWTON = 2
BOTH = ("strike", "dip")
F32, BF16 = jnp.float32, jnp.bfloat16


def split(value):
    high = value.astype(BF16)
    low = (value - high.astype(F32)).astype(BF16)
    return high, low


def split_table(table):
    table = np.asarray(table, np.float64)
    high = table.astype(np.float32).astype(jnp.bfloat16)
    low = (table - high.astype(np.float64)).astype(np.float32).astype(jnp.bfloat16)
    return np.stack([high, low])


def dft_table():
    index = np.arange(DEV)
    angle = 2 * np.pi * (np.outer(index, index) % DEV) / DEV
    return split_table(np.concatenate([np.cos(angle), np.sin(angle)], 0))


def inner_table(sign):
    angle = 2 * np.pi * (np.outer(np.arange(ROWS), np.arange(ROWS)) % ROWS) / ROWS
    cos, sin = np.cos(angle) / math.sqrt(NX), sign * np.sin(angle) / math.sqrt(NX)
    table = np.zeros((2, ROWS, MODES, 2, MODES, ROWS))
    for m in range(MODES):
        table[0, :, m, 0, m, :] = cos
        table[0, :, m, 1, m, :] = -sin
        table[1, :, m, 0, m, :] = sin
        table[1, :, m, 1, m, :] = cos
    return table.reshape(128, 128)


def inverse_inner():
    forward = inner_table(-1.0).reshape(2, ROWS, MODES, 2, MODES, ROWS)
    return forward.transpose(3, 4, 5, 0, 1, 2).reshape(128, 128)


def twist_table():
    angle = 2 * np.pi * np.outer(np.arange(ROWS), np.arange(DEV)) / NX
    return np.concatenate([np.cos(angle), np.sin(angle)]).astype(np.float32)


def turn_table():
    angle = 2 * np.pi * np.outer(np.arange(MODES), np.arange(DEV)) / NZ
    table = np.stack([np.cos(angle), np.sin(angle)]) / math.sqrt(NZ)
    return table.reshape(2 * MODES, DEV).astype(np.float32)


def matrix_tables():
    dft = dft_table().reshape(4 * DEV, DEV)
    sides = [split_table(t) for t in (inner_table(-1.0), inverse_inner())]
    return np.concatenate([dft] + [np.concatenate([t[0], t[1]], 1) for t in sides], 0)


def angle_tables():
    return np.concatenate([twist_table(), turn_table()], 0)


def dot3(left, right):
    lh, ll = left
    rh, rl = right
    out = jnp.dot(lh, rh, preferred_element_type=F32)
    out += jnp.dot(ll, rh, preferred_element_type=F32)
    out += jnp.dot(lh, rl, preferred_element_type=F32)
    return out


def long_dft(blocks, mats, sign):
    rows = []
    for real, imag in blocks:
        if sign < 0:
            rows.append(jnp.concatenate([real, imag], 1))
            rows.append(jnp.concatenate([imag, -real], 1))
        else:
            rows.append(jnp.concatenate([real, -imag], 1))
            rows.append(jnp.concatenate([imag, real], 1))
    table = (mats[: 2 * DEV, :], mats[2 * DEV : 4 * DEV, :])
    out = dot3(split(jnp.concatenate(rows, 0)), table)
    return [
        (out[128 * c : 128 * c + 64], out[128 * c + 64 : 128 * c + 128])
        for c in range(len(blocks))
    ]


def read_lines(ref, which, count):
    blocks = []
    for c in which:
        lines = ref[pl.ds(c, DEV, stride=count), :].T
        blocks.append((lines[:64], lines[64:]))
    return blocks


def write_lines(ref, blocks):
    for c, (real, imag) in enumerate(blocks):
        ref[pl.ds(c, DEV, stride=len(blocks)), :] = jnp.concatenate([real, imag], 0).T


def turns(angles):
    cos = [angles[32 + m : 33 + m, :] for m in range(4)]
    sin = [angles[36 + m : 37 + m, :] for m in range(4)]
    return cos, sin


def dip_forward(field, angles):
    cos, sin = turns(angles)
    blocks = []
    for x0, x1, x2, x3 in field:
        even, odd, f, g = x0 + x2, x1 + x3, x0 - x2, x1 - x3
        y0, y2 = even + odd, even - odd
        real = [y0 * cos[0], f * cos[1] - g * sin[1], y2 * cos[2], f * cos[3] + g * sin[3]]
        imag = [
            jnp.zeros_like(y0),
            -(f * sin[1] + g * cos[1]),
            -(y2 * sin[2]),
            g * cos[3] - f * sin[3],
        ]
        blocks.append((jnp.concatenate(real, 0), jnp.concatenate(imag, 0)))
    return blocks


def dip_inverse(blocks, angles):
    cos, sin = turns(angles)
    field = []
    for real, imag in blocks:
        re = [real[16 * m : 16 * m + 16] for m in range(4)]
        im = [imag[16 * m : 16 * m + 16] for m in range(4)]
        u = [cos[m] * re[m] - sin[m] * im[m] for m in range(4)]
        v1 = cos[1] * im[1] + sin[1] * re[1]
        v3 = cos[3] * im[3] + sin[3] * re[3]
        a, b, c, d = u[0] + u[2], u[0] - u[2], u[1] + u[3], v3 - v1
        field.append(jnp.concatenate([a + c, b + d, a - c, b - d], 0))
    return field


def friction(force, prestress, strength, state):
    load_strike = prestress[0] + force[0]
    load_dip = prestress[1] + force[1]
    traction = jnp.sqrt(load_strike * load_strike + load_dip * load_dip)
    factor = jnp.exp(-state)
    ratio = traction / factor
    estimate = jnp.minimum(traction / strength, jnp.log(ratio + jnp.sqrt(ratio * ratio + 1.0)))
    half = 0.5 * factor
    for _ in range(NEWTON):
        up, down = jnp.exp(estimate), jnp.exp(-estimate)
        residual = traction - strength * estimate - half * (up - down)
        estimate = estimate + residual / (strength + half * (up + down))
    slip_speed = 2.0 * (traction - strength * estimate)
    scale = slip_speed / jnp.maximum(traction, 1.0)
    rates = [scale * load_strike, scale * load_dip]
    return rates, state + 0.5 * (factor - 0.5 * slip_speed)


def pack_slip_kernel(slip, out):
    for d in range(4):
        for c in range(3):
            out[d, 16 * c : 16 * c + 16, :] = slip[c, 16 * d : 16 * d + 16, :]


def pack_rest_kernel(prestress, normal, effect, state, *outs):
    own = lax.axis_index("dip")
    for i, out in enumerate(outs):
        rows = pl.ds(pl.multiple_of(lax.rem(own + i, 4) * 16, 16), 16)
        for c in range(2):
            out[16 * c : 16 * c + 16, :] = prestress[c, rows, :]
        out[32:48, :] = normal[rows, :] * effect[rows, :]
        out[48:64, :] = state[rows, :]


def first_kernel(fields, angles, mats, out):
    field = [[fields[d, 16 * c : 16 * c + 16, :] for d in range(4)] for c in range(3)]
    write_lines(out, long_dft(dip_forward(field, angles), mats, -1))


def middle_kernel(lines, part0, part1, part2, part3, angles, mats, out, state_out, fields):
    own = lax.axis_index("dip")
    for i, part in enumerate((part0, part1, part2, part3)):
        rows = pl.ds(pl.multiple_of(lax.rem(own + 4 - i, 4) * 16, 16), 16)
        for c in range(3):
            fields[c, rows, :] = part[16 * c : 16 * c + 16, :]
        state_out[rows, :] = part[48:64, :]
    force = dip_inverse(long_dft(read_lines(lines, (0, 1), 3), mats, 1), angles)
    rates, state = friction(force, (fields[0], fields[1]), fields[2], state_out[...])
    state_out[...] = state
    field = [[r[16 * d : 16 * d + 16] for d in range(4)] for r in rates]
    write_lines(out, long_dft(dip_forward(field, angles), mats, -1))


def opening_kernel(lines, angles, mats, out):
    out[...] = 2.0 * dip_inverse(long_dft(read_lines(lines, (2,), 3), mats, 1), angles)[0]


def last_kernel(lines, fields, state_in, opening, angles, mats, out):
    force = dip_inverse(long_dft(read_lines(lines, (0, 1), 2), mats, 1), angles)
    rates, state = friction(force, (fields[0], fields[1]), fields[2], state_in[...])
    for d in range(4):
        for c, value in enumerate(rates + [opening, state]):
            out[d, 16 * c : 16 * c + 16, :] = value[16 * d : 16 * d + 16, :]


def unpack_kernel(gathered, rates, state):
    for d in range(4):
        rows = slice(16 * d, 16 * d + 16)
        for c in range(3):
            rates[c, rows, :] = gathered[d, 16 * c : 16 * c + 16, :]
        state[rows, :] = gathered[d, 48:64, :]


def mixing(device):
    shape = (64, DEV)
    row = lax.broadcasted_iota(jnp.int32, shape, 0)
    kx = (row >> 2) * DEV + lax.broadcasted_iota(jnp.int32, shape, 1)
    kz = device * MODES + (row & 3)
    mz = jnp.where(2 * kz < NZ, kz, kz - NZ)
    mx = jnp.where(2 * kx < NX, kx, kx - NX)
    qz = mz.astype(F32) * (2.0 * math.pi / NZ)
    qx = mx.astype(F32) * (2.0 * math.pi / NX)
    q = jnp.sqrt(qx * qx + qz * qz)
    anchor = (mz == 0) & (mx == 0)
    safe = jnp.where(anchor, 1.0, q)
    ex = jnp.where(anchor, 1.0, qx / safe)
    ez = jnp.where(anchor, 0.0, qz / safe)
    xx, xz, zz = ex * ex, ex * ez, ez * ez
    decay = jnp.exp(-0.025 * q)
    envelope = -0.25 * q
    first = [jnp.cos(0.5 * s * q) for s in (1.0, 0.6, 1.7)]
    before = [jnp.ones(shape, F32)] * 3
    now = first
    out = []
    for lag in range(4):
        envelope = envelope * decay
        two, three, one = [envelope * c for c in now]
        out.append((xx * two + zz * three, xz * (two - three), zz * two + xx * three, one))
        now, before = [2.0 * f * c - p for f, c, p in zip(first, now, before)], now
    return out


def history_kernel(history, lengths, past1, past2, coef, held, reach):
    device = lax.axis_index("strike") * 4 + lax.axis_index("dip")
    for k1 in range(16):
        lanes = slice(DEV * k1, DEV * k1 + DEV)
        rows = slice(4 * k1, 4 * k1 + 4)
        reach[rows, :] = lengths[:, lanes].astype(F32)
    for lag in range(3):
        for c in range(3):
            for part in range(2):
                line = history[lag, c, part].astype(F32)
                for k1 in range(16):
                    held[lag, c, part, 4 * k1 : 4 * k1 + 4, :] = line[:, DEV * k1 : DEV * k1 + DEV]
    mix = mixing(device)
    length = reach[...]
    masked = [None] + [
        [jnp.where(length > float(lag), m, 0.0) for m in mix[lag]] for lag in range(1, 4)
    ]
    twice = 2.0 * mix[0][3]
    for i in range(3):
        coef[i] = mix[0][i]
        coef[4 + i] = masked[1][i]
    coef[3] = twice * mix[0][3] + masked[1][3]
    for part in range(2):
        rows = slice(64 * part, 64 * part + 64)
        totals = []
        for skip in (1, 2):
            total = [0.0, 0.0, 0.0]
            for lag in range(skip, 4):
                ss, sd, dd, op = masked[lag]
                a, b, c = [held[lag - skip, i, part] for i in range(3)]
                total[0] = total[0] + (ss * a + sd * b)
                total[1] = total[1] + (sd * a + dd * b)
                total[2] = total[2] + op * c
            totals.append(total)
        for i in range(2):
            past1[i, rows, :] = totals[0][i]
            past2[i, rows, :] = totals[1][i]
        past1[2, rows, :] = twice * totals[0][2] + totals[1][2]


def spectrum_of(blocks, angles, mats):
    blocks = long_dft(blocks, mats, -1)
    cos = jnp.concatenate([angles[0:16, :]] * 4, 0)
    sin = jnp.concatenate([angles[16:32, :]] * 4, 0)
    turned = [
        jnp.concatenate([re * cos + im * sin, im * cos - re * sin], 0) for re, im in blocks
    ]
    inner = (mats[1024:1152, :128], mats[1024:1152, 128:])
    return dot3(inner, split(jnp.concatenate(turned, 1)))


def lines_of(out, force, angles, mats):
    back = (mats[1152:1280, :128], mats[1152:1280, 128:])
    blocks = dot3(back, split(jnp.concatenate(force, 1)))
    cos = jnp.concatenate([angles[0:16, :]] * 4, 0)
    sin = jnp.concatenate([angles[16:32, :]] * 4, 0)
    turned = []
    for c in range(len(force)):
        re, im = blocks[:64, DEV * c : DEV * c + DEV], blocks[64:, DEV * c : DEV * c + DEV]
        turned.append((re * cos - im * sin, im * cos + re * sin))
    write_lines(out, long_dft(turned, mats, 1))


def both_parts(coef, i):
    return jnp.concatenate([coef[i]] * 2, 0)


def apply_mix(coef, at, spec):
    ss, sd, dd = [both_parts(coef, at + i) for i in range(3)]
    s, d = spec[:, :DEV], spec[:, DEV : 2 * DEV]
    return [ss * s + sd * d, sd * s + dd * d]


def mode_kernel_first(lines, past, coef, angles, mats, out, spec_out):
    spec = spectrum_of(read_lines(lines, (0, 1, 2), 3), angles, mats)
    spec_out[...] = spec[:, : 2 * DEV]
    force = apply_mix(coef, 0, spec) + [both_parts(coef, 3) * spec[:, 2 * DEV :]]
    lines_of(out, [f + past[c] for c, f in enumerate(force)], angles, mats)


def older_kernel(past, coef, spec, out):
    for c, f in enumerate(apply_mix(coef, 4, spec)):
        out[c] = f + past[c]


def mode_kernel_second(lines, older, coef, angles, mats, out):
    spec = spectrum_of(read_lines(lines, (0, 1), 2), angles, mats)
    force = apply_mix(coef, 0, spec)
    lines_of(out, [f + older[c] for c, f in enumerate(force)], angles, mats)


def call(kernel, outs, *args, scratch=(), grant=20, work=2.0):
    return pl.pallas_call(
        kernel,
        out_shape=[jax.ShapeDtypeStruct(s, F32) for s in outs],
        scratch_shapes=scratch,
        compiler_params=pltpu.CompilerParams(vmem_limit_bytes=grant << 20),
        cost_estimate=pl.CostEstimate(
            flops=int(work * 1e9), bytes_accessed=int(work * 3e6), transcendentals=0
        ),
    )(*args)


def exchange(lines):
    lanes = lines.shape[0] // DEV * 128
    swapped = lax.all_to_all(lines.reshape(DEV, 1, lanes), BOTH, 0, 0, tiled=True)
    return swapped.reshape(lines.shape)


def shards(slip_rate, history, lengths, prestress, normal_stress, direct_effect, state_log):
    mats, angles = matrix_tables(), angle_tables()
    three, two = (3 * DEV, 128), (2 * DEV, 128)
    (packed,) = call(pack_slip_kernel, [(4, 48, 256)], slip_rate, grant=60)
    slip = lax.all_to_all(packed, "dip", 0, 0, tiled=True)
    (out,) = call(first_kernel, [three], slip, angles, mats)
    lines = exchange(out)
    parts = call(
        pack_rest_kernel,
        [(64, 256)] * 4,
        prestress,
        normal_stress,
        direct_effect,
        state_log,
    )
    parts = [
        lax.ppermute(part, "dip", [(j, (j + i) % 4) for j in range(4)]) if i else part
        for i, part in enumerate(parts)
    ]
    past1, past2, coef = call(
        history_kernel,
        [(3, 128, 256), (2, 128, 256), (7, 64, 256)],
        history,
        lengths,
        scratch=[pltpu.VMEM((3, 3, 2, 64, 256), F32), pltpu.VMEM((64, 256), F32)],
    )
    out, spec = call(
        mode_kernel_first, [three, (128, 512)], lines, past1, coef, angles, mats
    )
    lines = exchange(out)
    (older,) = call(older_kernel, [(2, 128, 256)], past2, coef, spec)
    out, state, fields = call(
        middle_kernel, [two, (64, 256), (3, 64, 256)], lines, *parts, angles, mats
    )
    (opening,) = call(opening_kernel, [(64, 256)], lines, angles, mats)
    (out,) = call(mode_kernel_second, [two], exchange(out), older, coef, angles, mats)
    (out,) = call(
        last_kernel, [(4, 64, 256)], exchange(out), fields, state, opening, angles, mats
    )
    gathered = lax.all_to_all(out, "dip", 0, 0, tiled=True)
    rates, state = call(unpack_kernel, [(3, 64, 256), (64, 256)], gathered)
    return rates, state


def solution(mesh):
    return jax.shard_map(
        shards,
        mesh=mesh,
        in_specs=(
            P(None, "strike", "dip"),
            P(None, None, None, ("strike", "dip"), None),
            P(("strike", "dip"), None),
            P(None, "strike", "dip"),
            P("strike", "dip"),
            P("strike", "dip"),
            P("strike", "dip"),
        ),
        out_specs=(P(None, "strike", "dip"), P("strike", "dip")),
        check_vma=False,
    )
```

```python
import math

import jax
import jax.numpy as jnp
import numpy as np
from jax import lax
from jax.experimental import pallas as pl
from jax.experimental.pallas import tpu as pltpu
from jax.sharding import PartitionSpec as P

NX, NZ = 4096, 1024
DEV = 256
ROWS = NX // DEV
MODES = NZ // DEV
NEWTON = 2
BOTH = ("strike", "dip")
F32, BF16 = jnp.float32, jnp.bfloat16


def split(value):
    high = value.astype(BF16)
    low = (value - high.astype(F32)).astype(BF16)
    return high, low


def split_table(table):
    table = np.asarray(table, np.float64)
    high = table.astype(np.float32).astype(jnp.bfloat16)
    low = (table - high.astype(np.float64)).astype(np.float32).astype(jnp.bfloat16)
    return np.stack([high, low])


def dft_table():
    index = np.arange(DEV)
    angle = 2 * np.pi * (np.outer(index, index) % DEV) / DEV
    return split_table(np.concatenate([np.cos(angle), np.sin(angle)], 0))


def inner_table(sign):
    angle = 2 * np.pi * (np.outer(np.arange(ROWS), np.arange(ROWS)) % ROWS) / ROWS
    cos, sin = np.cos(angle) / math.sqrt(NX), sign * np.sin(angle) / math.sqrt(NX)
    table = np.zeros((2, ROWS, MODES, 2, MODES, ROWS))
    for m in range(MODES):
        table[0, :, m, 0, m, :] = cos
        table[0, :, m, 1, m, :] = -sin
        table[1, :, m, 0, m, :] = sin
        table[1, :, m, 1, m, :] = cos
    return table.reshape(128, 128)


def inverse_inner():
    forward = inner_table(-1.0).reshape(2, ROWS, MODES, 2, MODES, ROWS)
    return forward.transpose(3, 4, 5, 0, 1, 2).reshape(128, 128)


def twist_table():
    angle = 2 * np.pi * np.outer(np.arange(ROWS), np.arange(DEV)) / NX
    return np.concatenate([np.cos(angle), np.sin(angle)]).astype(np.float32)


def turn_table():
    angle = 2 * np.pi * np.outer(np.arange(MODES), np.arange(DEV)) / NZ
    table = np.stack([np.cos(angle), np.sin(angle)]) / math.sqrt(NZ)
    return table.reshape(2 * MODES, DEV).astype(np.float32)


def matrix_tables():
    dft = dft_table().reshape(4 * DEV, DEV)
    sides = [split_table(t) for t in (inner_table(-1.0), inverse_inner())]
    return np.concatenate([dft] + [np.concatenate([t[0], t[1]], 1) for t in sides], 0)


def angle_tables():
    return np.concatenate([twist_table(), turn_table()], 0)


def dot3(left, right):
    lh, ll = left
    rh, rl = right
    out = jnp.dot(lh, rh, preferred_element_type=F32)
    out += jnp.dot(ll, rh, preferred_element_type=F32)
    out += jnp.dot(lh, rl, preferred_element_type=F32)
    return out


def long_dft(blocks, mats, sign):
    rows = []
    for real, imag in blocks:
        if sign < 0:
            rows.append(jnp.concatenate([real, imag], 1))
            rows.append(jnp.concatenate([imag, -real], 1))
        else:
            rows.append(jnp.concatenate([real, -imag], 1))
            rows.append(jnp.concatenate([imag, real], 1))
    table = (mats[: 2 * DEV, :], mats[2 * DEV : 4 * DEV, :])
    out = dot3(split(jnp.concatenate(rows, 0)), table)
    return [
        (out[128 * c : 128 * c + 64], out[128 * c + 64 : 128 * c + 128])
        for c in range(len(blocks))
    ]


def read_lines(ref, which, count):
    blocks = []
    for c in which:
        lines = ref[pl.ds(c, DEV, stride=count), :].T
        blocks.append((lines[:64], lines[64:]))
    return blocks


def write_lines(ref, blocks):
    for c, (real, imag) in enumerate(blocks):
        ref[pl.ds(c, DEV, stride=len(blocks)), :] = jnp.concatenate([real, imag], 0).T


def turns(angles):
    cos = [angles[32 + m : 33 + m, :] for m in range(4)]
    sin = [angles[36 + m : 37 + m, :] for m in range(4)]
    return cos, sin


def dip_forward(field, angles):
    cos, sin = turns(angles)
    blocks = []
    for x0, x1, x2, x3 in field:
        even, odd, f, g = x0 + x2, x1 + x3, x0 - x2, x1 - x3
        y0, y2 = even + odd, even - odd
        real = [y0 * cos[0], f * cos[1] - g * sin[1], y2 * cos[2], f * cos[3] + g * sin[3]]
        imag = [
            jnp.zeros_like(y0),
            -(f * sin[1] + g * cos[1]),
            -(y2 * sin[2]),
            g * cos[3] - f * sin[3],
        ]
        blocks.append((jnp.concatenate(real, 0), jnp.concatenate(imag, 0)))
    return blocks


def dip_inverse(blocks, angles):
    cos, sin = turns(angles)
    field = []
    for real, imag in blocks:
        re = [real[16 * m : 16 * m + 16] for m in range(4)]
        im = [imag[16 * m : 16 * m + 16] for m in range(4)]
        u = [cos[m] * re[m] - sin[m] * im[m] for m in range(4)]
        v1 = cos[1] * im[1] + sin[1] * re[1]
        v3 = cos[3] * im[3] + sin[3] * re[3]
        a, b, c, d = u[0] + u[2], u[0] - u[2], u[1] + u[3], v3 - v1
        field.append(jnp.concatenate([a + c, b + d, a - c, b - d], 0))
    return field


def friction(force, prestress, strength, state):
    load_strike = prestress[0] + force[0]
    load_dip = prestress[1] + force[1]
    traction = jnp.sqrt(load_strike * load_strike + load_dip * load_dip)
    factor = jnp.exp(-state)
    ratio = traction / factor
    estimate = jnp.minimum(traction / strength, jnp.log(ratio + jnp.sqrt(ratio * ratio + 1.0)))
    half = 0.5 * factor
    for _ in range(NEWTON):
        up, down = jnp.exp(estimate), jnp.exp(-estimate)
        residual = traction - strength * estimate - half * (up - down)
        estimate = estimate + residual / (strength + half * (up + down))
    slip_speed = 2.0 * (traction - strength * estimate)
    scale = slip_speed / jnp.maximum(traction, 1.0)
    rates = [scale * load_strike, scale * load_dip]
    return rates, state + 0.5 * (factor - 0.5 * slip_speed)


def pack_rest_kernel(prestress, normal, effect, state, *outs):
    own = lax.axis_index("dip")
    for i, out in enumerate(outs):
        rows = pl.ds(pl.multiple_of(lax.rem(own + i, 4) * 16, 16), 16)
        for c in range(2):
            out[16 * c : 16 * c + 16, :] = prestress[c, rows, :]
        out[32:48, :] = normal[rows, :] * effect[rows, :]
        out[48:64, :] = state[rows, :]


def first_kernel(fields, angles, mats, out):
    field = [[fields[d, 16 * c : 16 * c + 16, :] for d in range(4)] for c in range(3)]
    write_lines(out, long_dft(dip_forward(field, angles), mats, -1))


def middle_kernel(lines, part0, part1, part2, part3, angles, mats, out, state_out, fields, opening):
    own = lax.axis_index("dip")
    for i, part in enumerate((part0, part1, part2, part3)):
        rows = pl.ds(pl.multiple_of(lax.rem(own + 4 - i, 4) * 16, 16), 16)
        for c in range(3):
            fields[c, rows, :] = part[16 * c : 16 * c + 16, :]
        state_out[rows, :] = part[48:64, :]
    force = dip_inverse(long_dft(read_lines(lines, (0, 1, 2), 3), mats, 1), angles)
    opening[...] = 2.0 * force[2]
    rates, state = friction(force, (fields[0], fields[1]), fields[2], state_out[...])
    state_out[...] = state
    field = [[r[16 * d : 16 * d + 16] for d in range(4)] for r in rates]
    write_lines(out, long_dft(dip_forward(field, angles), mats, -1))


def last_kernel(lines, fields, state_in, opening, angles, mats, out):
    force = dip_inverse(long_dft(read_lines(lines, (0, 1), 2), mats, 1), angles)
    rates, state = friction(force, (fields[0], fields[1]), fields[2], state_in[...])
    for d in range(4):
        for c, value in enumerate(rates + [opening, state]):
            out[d, 16 * c : 16 * c + 16, :] = value[16 * d : 16 * d + 16, :]


def unpack_kernel(gathered, rates, state):
    for d in range(4):
        rows = slice(16 * d, 16 * d + 16)
        for c in range(3):
            rates[c, rows, :] = gathered[d, 16 * c : 16 * c + 16, :]
        state[rows, :] = gathered[d, 48:64, :]


def mixing(device):
    shape = (64, DEV)
    row = lax.broadcasted_iota(jnp.int32, shape, 0)
    kx = (row >> 2) * DEV + lax.broadcasted_iota(jnp.int32, shape, 1)
    kz = device * MODES + (row & 3)
    mz = jnp.where(2 * kz < NZ, kz, kz - NZ)
    mx = jnp.where(2 * kx < NX, kx, kx - NX)
    qz = mz.astype(F32) * (2.0 * math.pi / NZ)
    qx = mx.astype(F32) * (2.0 * math.pi / NX)
    q = jnp.sqrt(qx * qx + qz * qz)
    anchor = (mz == 0) & (mx == 0)
    safe = jnp.where(anchor, 1.0, q)
    ex = jnp.where(anchor, 1.0, qx / safe)
    ez = jnp.where(anchor, 0.0, qz / safe)
    xx, xz, zz = ex * ex, ex * ez, ez * ez
    decay = jnp.exp(-0.025 * q)
    envelope = -0.25 * q
    first = [jnp.cos(0.5 * s * q) for s in (1.0, 0.6, 1.7)]
    before = [jnp.ones(shape, F32)] * 3
    now = first
    out = []
    for lag in range(4):
        envelope = envelope * decay
        two, three, one = [envelope * c for c in now]
        out.append((xx * two + zz * three, xz * (two - three), zz * two + xx * three, one))
        now, before = [2.0 * f * c - p for f, c, p in zip(first, now, before)], now
    return out


def history_kernel(history, lengths, past1, past2, coef, held, reach):
    device = lax.axis_index("strike") * 4 + lax.axis_index("dip")
    for k1 in range(16):
        lanes = slice(DEV * k1, DEV * k1 + DEV)
        rows = slice(4 * k1, 4 * k1 + 4)
        reach[rows, :] = lengths[:, lanes].astype(F32)
    for lag in range(3):
        for c in range(3):
            for part in range(2):
                line = history[lag, c, part].astype(F32)
                for k1 in range(16):
                    held[lag, c, part, 4 * k1 : 4 * k1 + 4, :] = line[:, DEV * k1 : DEV * k1 + DEV]
    mix = mixing(device)
    length = reach[...]
    masked = [None] + [
        [jnp.where(length > float(lag), m, 0.0) for m in mix[lag]] for lag in range(1, 4)
    ]
    twice = 2.0 * mix[0][3]
    for i in range(3):
        coef[i] = mix[0][i]
        coef[4 + i] = masked[1][i]
    coef[3] = twice * mix[0][3] + masked[1][3]
    for part in range(2):
        rows = slice(64 * part, 64 * part + 64)
        totals = []
        for skip in (1, 2):
            total = [0.0, 0.0, 0.0]
            for lag in range(skip, 4):
                ss, sd, dd, op = masked[lag]
                a, b, c = [held[lag - skip, i, part] for i in range(3)]
                total[0] = total[0] + (ss * a + sd * b)
                total[1] = total[1] + (sd * a + dd * b)
                total[2] = total[2] + op * c
            totals.append(total)
        for i in range(2):
            past1[i, rows, :] = totals[0][i]
            past2[i, rows, :] = totals[1][i]
        past1[2, rows, :] = twice * totals[0][2] + totals[1][2]


def spectrum_of(blocks, angles, mats):
    blocks = long_dft(blocks, mats, -1)
    cos = jnp.concatenate([angles[0:16, :]] * 4, 0)
    sin = jnp.concatenate([angles[16:32, :]] * 4, 0)
    turned = [
        jnp.concatenate([re * cos + im * sin, im * cos - re * sin], 0) for re, im in blocks
    ]
    inner = (mats[1024:1152, :128], mats[1024:1152, 128:])
    return dot3(inner, split(jnp.concatenate(turned, 1)))


def lines_of(out, force, angles, mats):
    back = (mats[1152:1280, :128], mats[1152:1280, 128:])
    blocks = dot3(back, split(jnp.concatenate(force, 1)))
    cos = jnp.concatenate([angles[0:16, :]] * 4, 0)
    sin = jnp.concatenate([angles[16:32, :]] * 4, 0)
    turned = []
    for c in range(len(force)):
        re, im = blocks[:64, DEV * c : DEV * c + DEV], blocks[64:, DEV * c : DEV * c + DEV]
        turned.append((re * cos - im * sin, im * cos + re * sin))
    write_lines(out, long_dft(turned, mats, 1))


def both_parts(coef, i):
    return jnp.concatenate([coef[i]] * 2, 0)


def apply_mix(coef, at, spec):
    ss, sd, dd = [both_parts(coef, at + i) for i in range(3)]
    s, d = spec[:, :DEV], spec[:, DEV : 2 * DEV]
    return [ss * s + sd * d, sd * s + dd * d]


def mode_kernel_first(lines, past, past_next, coef, angles, mats, out, older):
    spec = spectrum_of(read_lines(lines, (0, 1, 2), 3), angles, mats)
    for c, f in enumerate(apply_mix(coef, 4, spec)):
        older[c] = f + past_next[c]
    force = apply_mix(coef, 0, spec) + [both_parts(coef, 3) * spec[:, 2 * DEV :]]
    lines_of(out, [f + past[c] for c, f in enumerate(force)], angles, mats)


def mode_kernel_second(lines, older, coef, angles, mats, out):
    spec = spectrum_of(read_lines(lines, (0, 1), 2), angles, mats)
    force = apply_mix(coef, 0, spec)
    lines_of(out, [f + older[c] for c, f in enumerate(force)], angles, mats)


def call(kernel, outs, *args, scratch=(), grant=20, work=2.0):
    return pl.pallas_call(
        kernel,
        out_shape=[jax.ShapeDtypeStruct(s, F32) for s in outs],
        scratch_shapes=scratch,
        compiler_params=pltpu.CompilerParams(vmem_limit_bytes=grant << 20),
        cost_estimate=pl.CostEstimate(
            flops=int(work * 1e9), bytes_accessed=int(work * 3e6), transcendentals=0
        ),
    )(*args)


def exchange(lines):
    lanes = lines.shape[0] // DEV * 128
    swapped = lax.all_to_all(lines.reshape(DEV, 1, lanes), BOTH, 0, 0, tiled=True)
    return swapped.reshape(lines.shape)


def shards(slip_rate, history, lengths, prestress, normal_stress, direct_effect, state_log):
    mats, angles = matrix_tables(), angle_tables()
    three, two = (3 * DEV, 128), (2 * DEV, 128)
    packed = slip_rate.reshape(3, 4, 16, 256).transpose(1, 0, 2, 3).reshape(4, 48, 256)
    slip = lax.all_to_all(packed, "dip", 0, 0, tiled=True)
    (out,) = call(first_kernel, [three], slip, angles, mats)
    lines = exchange(out)
    parts = call(
        pack_rest_kernel,
        [(64, 256)] * 4,
        prestress,
        normal_stress,
        direct_effect,
        state_log,
    )
    parts = [
        lax.ppermute(part, "dip", [(j, (j + i) % 4) for j in range(4)]) if i else part
        for i, part in enumerate(parts)
    ]
    past1, past2, coef = call(
        history_kernel,
        [(3, 128, 256), (2, 128, 256), (7, 64, 256)],
        history,
        lengths,
        scratch=[pltpu.VMEM((3, 3, 2, 64, 256), F32), pltpu.VMEM((64, 256), F32)],
    )
    lines, parts, past1, past2, coef = lax.optimization_barrier(
        (lines, parts, past1, past2, coef)
    )
    out, older = call(
        mode_kernel_first, [three, (2, 128, 256)], lines, past1, past2, coef, angles, mats
    )
    out, state, fields, opening = call(
        middle_kernel,
        [two, (64, 256), (3, 64, 256), (64, 256)],
        exchange(out),
        *parts,
        angles,
        mats,
    )
    (out,) = call(mode_kernel_second, [two], exchange(out), older, coef, angles, mats)
    (out,) = call(
        last_kernel, [(4, 64, 256)], exchange(out), fields, state, opening, angles, mats
    )
    gathered = lax.all_to_all(out, "dip", 0, 0, tiled=True)
    rates, state = call(unpack_kernel, [(3, 64, 256), (64, 256)], gathered)
    return rates, state


def solution(mesh):
    return jax.shard_map(
        shards,
        mesh=mesh,
        in_specs=(
            P(None, "strike", "dip"),
            P(None, None, None, ("strike", "dip"), None),
            P(("strike", "dip"), None),
            P(None, "strike", "dip"),
            P("strike", "dip"),
            P("strike", "dip"),
            P("strike", "dip"),
        ),
        out_specs=(P(None, "strike", "dip"), P("strike", "dip")),
        check_vma=False,
    )
```

```python
import math

import jax
import jax.numpy as jnp
import numpy as np
from jax import lax
from jax.experimental import pallas as pl
from jax.experimental.pallas import tpu as pltpu
from jax.sharding import PartitionSpec as P

NX, NZ = 4096, 1024
DEV = 256
ROWS = NX // DEV
MODES = NZ // DEV
NEWTON = 2
BOTH = ("strike", "dip")
F32, BF16 = jnp.float32, jnp.bfloat16


def split(value):
    high = value.astype(BF16)
    low = (value - high.astype(F32)).astype(BF16)
    return high, low


def split_table(table):
    table = np.asarray(table, np.float64)
    high = table.astype(np.float32).astype(jnp.bfloat16)
    low = (table - high.astype(np.float64)).astype(np.float32).astype(jnp.bfloat16)
    return np.stack([high, low])


def dft_table():
    index = np.arange(DEV)
    angle = 2 * np.pi * (np.outer(index, index) % DEV) / DEV
    return split_table(np.concatenate([np.cos(angle), np.sin(angle)], 0))


def inner_table(sign):
    angle = 2 * np.pi * (np.outer(np.arange(ROWS), np.arange(ROWS)) % ROWS) / ROWS
    cos, sin = np.cos(angle) / math.sqrt(NX), sign * np.sin(angle) / math.sqrt(NX)
    table = np.zeros((2, ROWS, MODES, 2, MODES, ROWS))
    for m in range(MODES):
        table[0, :, m, 0, m, :] = cos
        table[0, :, m, 1, m, :] = -sin
        table[1, :, m, 0, m, :] = sin
        table[1, :, m, 1, m, :] = cos
    return table.reshape(128, 128)


def inverse_inner():
    forward = inner_table(-1.0).reshape(2, ROWS, MODES, 2, MODES, ROWS)
    return forward.transpose(3, 4, 5, 0, 1, 2).reshape(128, 128)


def twist_table():
    angle = 2 * np.pi * np.outer(np.arange(ROWS), np.arange(DEV)) / NX
    return np.concatenate([np.cos(angle), np.sin(angle)]).astype(np.float32)


def turn_table():
    angle = 2 * np.pi * np.outer(np.arange(MODES), np.arange(DEV)) / NZ
    table = np.stack([np.cos(angle), np.sin(angle)]) / math.sqrt(NZ)
    return table.reshape(2 * MODES, DEV).astype(np.float32)


def flip_tables():
    lanes = np.zeros((DEV, DEV))
    lanes[np.arange(DEV), -np.arange(DEV) % DEV] = 1.0
    rows = np.zeros((2, ROWS, MODES, DEV))
    for k1 in range(ROWS):
        for m in range(MODES):
            rows[0, k1, m, (15 - k1) * MODES + m] = 1.0
            rows[1, k1, m, (-k1 % ROWS) * MODES + m] = 1.0
    table = np.concatenate([lanes, rows.reshape(128, DEV)], 0)
    return table.astype(np.float32).astype(jnp.bfloat16)


def matrix_tables():
    dft = dft_table().reshape(4 * DEV, DEV)
    sides = [split_table(t) for t in (inner_table(-1.0), inverse_inner())]
    sides = [np.concatenate([t[0], t[1]], 1) for t in sides]
    return np.concatenate([dft] + sides + [flip_tables()], 0)


def angle_tables():
    return np.concatenate([twist_table(), turn_table()], 0)


def dot3(left, right):
    lh, ll = left
    rh, rl = right
    out = jnp.dot(lh, rh, preferred_element_type=F32)
    out += jnp.dot(ll, rh, preferred_element_type=F32)
    out += jnp.dot(lh, rl, preferred_element_type=F32)
    return out


def long_dft(blocks, mats, sign):
    rows = []
    for real, imag in blocks:
        if sign < 0:
            rows.append(jnp.concatenate([real, imag], 1))
            rows.append(jnp.concatenate([imag, -real], 1))
        else:
            rows.append(jnp.concatenate([real, -imag], 1))
            rows.append(jnp.concatenate([imag, real], 1))
    table = (mats[: 2 * DEV, :], mats[2 * DEV : 4 * DEV, :])
    out = dot3(split(jnp.concatenate(rows, 0)), table)
    return [
        (out[128 * c : 128 * c + 64], out[128 * c + 64 : 128 * c + 128])
        for c in range(len(blocks))
    ]


def read_lines(ref, which, count):
    blocks = []
    for c in which:
        lines = ref[pl.ds(c, DEV, stride=count), :].T
        blocks.append((lines[:64], lines[64:]))
    return blocks


def write_lines(ref, blocks):
    for c, (real, imag) in enumerate(blocks):
        ref[pl.ds(c, DEV, stride=len(blocks)), :] = jnp.concatenate([real, imag], 0).T


def position():
    return lax.axis_index("strike") * 4 + lax.axis_index("dip")


def send_half(ref, field, angles, mats):
    halves = ([], [])
    lasts = []
    lane = lax.broadcasted_iota(jnp.int32, (16, DEV), 1)
    sign = 1.0 - 2.0 * (lane & 1).astype(F32)
    for real, imag in dip_forward(field, angles):
        lasts.append(jnp.sum(real[:16] * sign, 1, keepdims=True))
        for rows, at in zip(halves, (0, 16)):
            re, im = real[at : at + 32], imag[at : at + 32]
            rows.append(jnp.concatenate([re, im], 1))
            rows.append(jnp.concatenate([im, -re], 1))
    outs = []
    for rows, lanes in zip(halves, (slice(0, 128), slice(128, 256))):
        table = (mats[: 2 * DEV, lanes], mats[2 * DEV : 4 * DEV, lanes])
        outs.append(dot3(split(jnp.concatenate(rows, 0)), table))
    out = jnp.concatenate(outs, 1)
    pieces = []
    for c, last in enumerate(lasts):
        pieces.append(out[64 * c : 64 * c + 32])
        pieces.append(jnp.where(lane == 0, last, out[64 * c + 32 : 64 * c + 48]))
        pieces.append(out[64 * c + 48 : 64 * c + 64])
    if len(lasts) == 2:
        ref[...] = jnp.concatenate(pieces, 0).T
    else:
        ref[pl.ds(0, DEV, stride=2), :] = jnp.concatenate(pieces[:6], 0).T
        pieces.append(jnp.zeros((64, DEV), F32))
        ref[pl.ds(1, DEV, stride=2), :] = jnp.concatenate(pieces[6:], 0).T


def receive_half(ref, count):
    device = position()
    low = jnp.where(device < DEV // 2, 1.0, 0.0)
    zero = jnp.where(device == 0, 1.0, 0.0)
    up = 1.0 - low
    if count == 2:
        lines = [ref[...].T]
    else:
        lines = [ref[pl.ds(i, DEV, stride=2), :].T for i in range(2)]
    blocks = []
    for c in range(count):
        line = lines[c // 2][64 * (c % 2) : 64 * (c % 2) + 64]
        ar, br, ai, bi = [line[16 * i : 16 * i + 16] for i in range(4)]
        none = jnp.zeros_like(ar)
        real = [low * ar, low * br + up * ar, up * br + zero * ai, none]
        imag = [(low - zero) * ai, low * bi + up * ai, up * bi, none]
        blocks.append((jnp.concatenate(real, 0), jnp.concatenate(imag, 0)))
    return blocks


def turns(angles):
    cos = [angles[32 + m : 33 + m, :] for m in range(4)]
    sin = [angles[36 + m : 37 + m, :] for m in range(4)]
    return cos, sin


def dip_forward(field, angles):
    cos, sin = turns(angles)
    blocks = []
    for x0, x1, x2, x3 in field:
        even, odd, f, g = x0 + x2, x1 + x3, x0 - x2, x1 - x3
        y0, y2 = even + odd, even - odd
        real = [y0 * cos[0], f * cos[1] - g * sin[1], y2 * cos[2], f * cos[3] + g * sin[3]]
        imag = [
            jnp.zeros_like(y0),
            -(f * sin[1] + g * cos[1]),
            -(y2 * sin[2]),
            g * cos[3] - f * sin[3],
        ]
        blocks.append((jnp.concatenate(real, 0), jnp.concatenate(imag, 0)))
    return blocks


def dip_inverse(lines, angles, mats):
    lasts = [imag[:16, :1] for _, imag in lines]
    blocks = long_dft(lines, mats, 1)
    cos, sin = turns(angles)
    lane = lax.broadcasted_iota(jnp.int32, (16, DEV), 1)
    sign = (1.0 - 2.0 * (lane & 1).astype(F32)) * (1.0 / math.sqrt(NZ))
    field = []
    for (real, imag), last in zip(blocks, lasts):
        re = [real[16 * m : 16 * m + 16] for m in range(4)]
        im = [imag[16 * m : 16 * m + 16] for m in range(4)]
        u = [cos[m] * re[m] - sin[m] * im[m] for m in range(4)]
        v1 = cos[1] * im[1] + sin[1] * re[1]
        v3 = cos[3] * im[3] + sin[3] * re[3]
        a, b, c, d = u[0] + u[2], u[0] - u[2], u[1] + u[3], v3 - v1
        a, b = a + sign * last, b + sign * last
        field.append(jnp.concatenate([a + c, b + d, a - c, b - d], 0))
    return field


def friction(force, prestress, strength, state):
    load_strike = prestress[0] + force[0]
    load_dip = prestress[1] + force[1]
    traction = jnp.sqrt(load_strike * load_strike + load_dip * load_dip)
    factor = jnp.exp(-state)
    ratio = traction / factor
    estimate = jnp.minimum(traction / strength, jnp.log(ratio + jnp.sqrt(ratio * ratio + 1.0)))
    half = 0.5 * factor
    for _ in range(NEWTON):
        up, down = jnp.exp(estimate), jnp.exp(-estimate)
        residual = traction - strength * estimate - half * (up - down)
        estimate = estimate + residual / (strength + half * (up + down))
    slip_speed = 2.0 * (traction - strength * estimate)
    scale = slip_speed / jnp.maximum(traction, 1.0)
    rates = [scale * load_strike, scale * load_dip]
    return rates, state + 0.5 * (factor - 0.5 * slip_speed)


def pack_rest_kernel(prestress, normal, effect, state, *outs):
    own = lax.axis_index("dip")
    for i, out in enumerate(outs):
        rows = pl.ds(pl.multiple_of(lax.rem(own + i, 4) * 16, 16), 16)
        for c in range(2):
            out[16 * c : 16 * c + 16, :] = prestress[c, rows, :]
        out[32:48, :] = normal[rows, :] * effect[rows, :]
        out[48:64, :] = state[rows, :]


def first_kernel(fields, angles, mats, out):
    field = [[fields[d, 16 * c : 16 * c + 16, :] for d in range(4)] for c in range(3)]
    send_half(out, field, angles, mats)


def middle_kernel(lines, part0, part1, part2, part3, angles, mats, out, state_out, fields, opening):
    own = lax.axis_index("dip")
    for i, part in enumerate((part0, part1, part2, part3)):
        rows = pl.ds(pl.multiple_of(lax.rem(own + 4 - i, 4) * 16, 16), 16)
        for c in range(3):
            fields[c, rows, :] = part[16 * c : 16 * c + 16, :]
        state_out[rows, :] = part[48:64, :]
    force = dip_inverse(read_lines(lines, (0, 1, 2), 3), angles, mats)
    opening[...] = 2.0 * force[2]
    rates, state = friction(force, (fields[0], fields[1]), fields[2], state_out[...])
    state_out[...] = state
    field = [[r[16 * d : 16 * d + 16] for d in range(4)] for r in rates]
    send_half(out, field, angles, mats)


def last_kernel(lines, fields, state_in, opening, angles, mats, out):
    force = dip_inverse(read_lines(lines, (0, 1), 2), angles, mats)
    rates, state = friction(force, (fields[0], fields[1]), fields[2], state_in[...])
    for d in range(4):
        for c, value in enumerate(rates + [opening, state]):
            out[d, 16 * c : 16 * c + 16, :] = value[16 * d : 16 * d + 16, :]


def unpack_kernel(gathered, rates, state):
    for d in range(4):
        rows = slice(16 * d, 16 * d + 16)
        for c in range(3):
            rates[c, rows, :] = gathered[d, 16 * c : 16 * c + 16, :]
        state[rows, :] = gathered[d, 48:64, :]


def mixing(kz, kx, lags):
    shape = kz.shape
    mz = jnp.where(2 * kz < NZ, kz, kz - NZ)
    mx = jnp.where(2 * kx < NX, kx, kx - NX)
    qz = mz.astype(F32) * (2.0 * math.pi / NZ)
    qx = mx.astype(F32) * (2.0 * math.pi / NX)
    q = jnp.sqrt(qx * qx + qz * qz)
    anchor = (mz == 0) & (mx == 0)
    safe = jnp.where(anchor, 1.0, q)
    ex = jnp.where(anchor, 1.0, qx / safe)
    ez = jnp.where(anchor, 0.0, qz / safe)
    xx, xz, zz = ex * ex, ex * ez, ez * ez
    decay = jnp.exp(-0.025 * q)
    envelope = -0.25 * q
    first = [jnp.cos(0.5 * s * q) for s in (1.0, 0.6, 1.7)]
    before = [jnp.ones(shape, F32)] * 3
    now = first
    out = []
    for _ in range(lags):
        envelope = envelope * decay
        two, three, one = [envelope * c for c in now]
        out.append((xx * two + zz * three, xz * (two - three), zz * two + xx * three, one))
        now, before = [2.0 * f * c - p for f, c, p in zip(first, now, before)], now
    return out


def spread(lengths):
    line = lengths[...].astype(F32)
    return jnp.concatenate([line[:, DEV * k1 : DEV * k1 + DEV] for k1 in range(16)], 0)


def flip(arrays, mats):
    lanes, rows = mats[1280:1536, :], (mats[1536:1600, :64], mats[1600:1664, :64])
    first = lax.broadcasted_iota(jnp.int32, (64, DEV), 1) == 0
    turned = sum(
        jnp.dot(part, lanes, preferred_element_type=F32)
        for part in split(jnp.concatenate(arrays, 0))
    )
    count = len(arrays)
    parts = split(jnp.concatenate([turned[64 * i : 64 * i + 64] for i in range(count)], 1))
    wide = [sum(jnp.dot(r, p, preferred_element_type=F32) for p in parts) for r in rows]
    return [
        jnp.where(first, *[w[:, DEV * i : DEV * i + DEV] for w in (wide[1], wide[0])])
        for i in range(count)
    ]


def history_kernel(history, lengths, across, beside, mats, past1, past2, coef, held):
    device = position()
    for lag in range(3):
        for c in range(3):
            for part in range(2):
                line = history[lag, c, part].astype(F32)
                for k1 in range(16):
                    held[lag, c, part, 4 * k1 : 4 * k1 + 4, :] = line[:, DEV * k1 : DEV * k1 + DEV]
    shape = (64, DEV)
    row = lax.broadcasted_iota(jnp.int32, shape, 0)
    kx = (row >> 2) * DEV + lax.broadcasted_iota(jnp.int32, shape, 1)
    m = row & 3
    zero = device == 0
    upper = jnp.where(device < DEV // 2, 0, 1)
    origin = jnp.where(zero, 0, 64)
    anchor = (m + origin) == 0
    guest = (m + origin) == 2
    length = spread(lengths)
    mix = mixing(device * MODES + m, kx, 4)
    masked = [None] + [
        [jnp.where(length > float(lag), v, 0.0) for v in mix[lag]] for lag in range(1, 4)
    ]

    def active(value):
        return jnp.where(value > 1.0, 1.0, 0.0)

    other = active(spread(beside))
    own = active(length)
    own_back, across_back, other_back = flip([own, active(spread(across)), other], mats)
    own = jnp.where(guest, pltpu.roll(other, 2, 0), own)
    back = jnp.where(m == 1, pltpu.roll(across_back, 62, 0), across_back)
    back = jnp.where(m == 0, other_back, back)
    back = jnp.where(anchor, own_back, back)
    back = jnp.where(guest, pltpu.roll(other_back, 2, 0), back)
    mine = (m == upper) | (m == upper + 1)
    weight = jnp.where(mine, 1.0, 0.0)
    weight = jnp.where(anchor | guest, 0.5, weight)
    nyquist = kx == NX // 2
    total, cross = own + back, jnp.where(nyquist, own - back, own + back)
    cross = jnp.where(guest, jnp.where(nyquist, total, own - back), cross)
    cross0 = jnp.where(nyquist, 0.0, 2.0 * weight)
    cross0 = jnp.where(guest, jnp.where(nyquist, 1.0, 0.0), cross0)
    new, old = mixing(jnp.where(guest, NZ // 2, device * MODES + m), kx, 2)
    coef[0] = 2.0 * weight * new[0]
    coef[1] = cross0 * new[1]
    coef[2] = 2.0 * weight * new[2]
    coef[3] = weight * (4.0 * new[3] * new[3] + total * old[3])
    coef[4] = weight * total * old[0]
    coef[5] = weight * cross * old[1]
    coef[6] = weight * total * old[2]
    coef[7] = jnp.where(guest, 1.0, 0.0)
    sums = []
    for part in range(2):
        totals = []
        for skip in (1, 2):
            value = [0.0, 0.0, 0.0]
            for lag in range(skip, 4):
                ss, sd, dd, op = masked[lag]
                a, b, c = [held[lag - skip, i, part] for i in range(3)]
                value[0] = value[0] + (ss * a + sd * b)
                value[1] = value[1] + (sd * a + dd * b)
                value[2] = value[2] + op * c
            totals.append(value)
        one, two = totals
        sums.append([one[0], one[1], 2.0 * mix[0][3] * one[2] + two[2], two[0], two[1]])
    turned = flip(sums[0] + sums[1], mats)
    for i in range(5):
        target = past1.at[i] if i < 3 else past2.at[i - 3]
        re, im = sums[0][i], sums[1][i]
        target[0:64, :] = jnp.where(anchor, 0.5 * (re + turned[i]), re)
        target[64:128, :] = jnp.where(anchor, 0.5 * (im - turned[5 + i]), im)


def spectrum_of(blocks, angles, mats):
    blocks = long_dft(blocks, mats, -1)
    cos = jnp.concatenate([angles[0:16, :]] * 4, 0)
    sin = jnp.concatenate([angles[16:32, :]] * 4, 0)
    turned = [
        jnp.concatenate([re * cos + im * sin, im * cos - re * sin], 0) for re, im in blocks
    ]
    inner = (mats[1024:1152, :128], mats[1024:1152, 128:])
    return dot3(inner, split(jnp.concatenate(turned, 1)))


def lines_of(out, force, angles, mats):
    back = (mats[1152:1280, :128], mats[1152:1280, 128:])
    blocks = dot3(back, split(jnp.concatenate(force, 1)))
    cos = jnp.concatenate([angles[0:16, :]] * 4, 0)
    sin = jnp.concatenate([angles[16:32, :]] * 4, 0)
    turned = []
    for c in range(len(force)):
        re, im = blocks[:64, DEV * c : DEV * c + DEV], blocks[64:, DEV * c : DEV * c + DEV]
        turned.append((re * cos - im * sin, im * cos + re * sin))
    write_lines(out, long_dft(turned, mats, 1))


def settle(coef, real, imag):
    guest = coef[7]
    gr, gi = guest * real, guest * imag
    real, imag = real - gr - pltpu.roll(gi, 62, 0), imag - gi + pltpu.roll(gr, 62, 0)
    return jnp.concatenate([real, imag], 0)


def apply_mix(coef, at, spec):
    out = [[], []]
    for rows in (slice(0, 64), slice(64, 128)):
        s, d = spec[rows, :DEV], spec[rows, DEV : 2 * DEV]
        out[0].append(coef[at] * s + coef[at + 1] * d)
        out[1].append(coef[at + 1] * s + coef[at + 2] * d)
    return [settle(coef, *parts) for parts in out]


def mode_kernel_first(lines, past, past_next, coef, angles, mats, out, older):
    spec = spectrum_of(receive_half(lines, 3), angles, mats)
    for c, f in enumerate(apply_mix(coef, 4, spec)):
        older[c] = f + past_next[c]
    opening = [coef[3] * spec[rows, 2 * DEV :] for rows in (slice(0, 64), slice(64, 128))]
    force = apply_mix(coef, 0, spec) + [settle(coef, *opening)]
    lines_of(out, [f + past[c] for c, f in enumerate(force)], angles, mats)


def mode_kernel_second(lines, older, coef, angles, mats, out):
    spec = spectrum_of(receive_half(lines, 2), angles, mats)
    force = apply_mix(coef, 0, spec)
    lines_of(out, [f + older[c] for c, f in enumerate(force)], angles, mats)


def call(kernel, outs, *args, scratch=(), grant=20, work=2.0):
    return pl.pallas_call(
        kernel,
        out_shape=[jax.ShapeDtypeStruct(s, F32) for s in outs],
        scratch_shapes=scratch,
        compiler_params=pltpu.CompilerParams(vmem_limit_bytes=grant << 20),
        cost_estimate=pl.CostEstimate(
            flops=int(work * 1e9), bytes_accessed=int(work * 3e6), transcendentals=0
        ),
    )(*args)


def exchange(lines):
    lanes = lines.shape[0] // DEV * 128
    swapped = lax.all_to_all(lines.reshape(DEV, 1, lanes), BOTH, 0, 0, tiled=True)
    return swapped.reshape(lines.shape)


def shards(slip_rate, history, lengths, prestress, normal_stress, direct_effect, state_log):
    mats, angles = matrix_tables(), angle_tables()
    three, two, one = (3 * DEV, 128), (2 * DEV, 128), (DEV, 128)
    across = lax.ppermute(lengths, BOTH, [(j, DEV - 1 - j) for j in range(DEV)])
    beside = [(DEV - j, j) for j in range(1, DEV // 2)] + [(DEV // 2, 0)]
    beside = lax.ppermute(lengths, BOTH, beside)
    packed = slip_rate.reshape(3, 4, 16, 256).transpose(1, 0, 2, 3).reshape(4, 48, 256)
    slip = lax.all_to_all(packed, "dip", 0, 0, tiled=True)
    (out,) = call(first_kernel, [two], slip, angles, mats)
    lines = exchange(out)
    parts = call(
        pack_rest_kernel,
        [(64, 256)] * 4,
        prestress,
        normal_stress,
        direct_effect,
        state_log,
    )
    parts = [
        lax.ppermute(part, "dip", [(j, (j + i) % 4) for j in range(4)]) if i else part
        for i, part in enumerate(parts)
    ]
    past1, past2, coef = call(
        history_kernel,
        [(3, 128, 256), (2, 128, 256), (8, 64, 256)],
        history,
        lengths,
        across,
        beside,
        mats,
        scratch=[pltpu.VMEM((3, 3, 2, 64, 256), F32)],
    )
    lines, parts, past1, past2, coef = lax.optimization_barrier(
        (lines, parts, past1, past2, coef)
    )
    out, older = call(
        mode_kernel_first, [three, (2, 128, 256)], lines, past1, past2, coef, angles, mats
    )
    out, state, fields, opening = call(
        middle_kernel,
        [one, (64, 256), (3, 64, 256), (64, 256)],
        exchange(out),
        *parts,
        angles,
        mats,
    )
    (out,) = call(mode_kernel_second, [two], exchange(out), older, coef, angles, mats)
    (out,) = call(
        last_kernel, [(4, 64, 256)], exchange(out), fields, state, opening, angles, mats
    )
    gathered = lax.all_to_all(out, "dip", 0, 0, tiled=True)
    rates, state = call(unpack_kernel, [(3, 64, 256), (64, 256)], gathered)
    return rates, state


def solution(mesh):
    return jax.shard_map(
        shards,
        mesh=mesh,
        in_specs=(
            P(None, "strike", "dip"),
            P(None, None, None, ("strike", "dip"), None),
            P(("strike", "dip"), None),
            P(None, "strike", "dip"),
            P("strike", "dip"),
            P("strike", "dip"),
            P("strike", "dip"),
        ),
        out_specs=(P(None, "strike", "dip"), P("strike", "dip")),
        check_vma=False,
    )
```

```python
import math

import jax
import jax.numpy as jnp
import numpy as np
from jax import lax
from jax.experimental import pallas as pl
from jax.experimental.pallas import tpu as pltpu
from jax.sharding import PartitionSpec as P

NX, NZ = 4096, 1024
DEV = 256
ROWS = NX // DEV
MODES = NZ // DEV
NEWTON = 2
BOTH = ("strike", "dip")
F32, BF16 = jnp.float32, jnp.bfloat16


def split(value):
    high = value.astype(BF16)
    low = (value - high.astype(F32)).astype(BF16)
    return high, low


def split_table(table):
    table = np.asarray(table, np.float64)
    high = table.astype(np.float32).astype(jnp.bfloat16)
    low = (table - high.astype(np.float64)).astype(np.float32).astype(jnp.bfloat16)
    return np.stack([high, low])


def dft_table():
    index = np.arange(DEV)
    angle = 2 * np.pi * (np.outer(index, index) % DEV) / DEV
    return split_table(np.concatenate([np.cos(angle), np.sin(angle)], 0))


def inner_table(sign):
    angle = 2 * np.pi * (np.outer(np.arange(ROWS), np.arange(ROWS)) % ROWS) / ROWS
    cos, sin = np.cos(angle) / math.sqrt(NX), sign * np.sin(angle) / math.sqrt(NX)
    table = np.zeros((2, ROWS, MODES, 2, MODES, ROWS))
    for m in range(MODES):
        table[0, :, m, 0, m, :] = cos
        table[0, :, m, 1, m, :] = -sin
        table[1, :, m, 0, m, :] = sin
        table[1, :, m, 1, m, :] = cos
    return table.reshape(128, 128)


def inverse_inner():
    forward = inner_table(-1.0).reshape(2, ROWS, MODES, 2, MODES, ROWS)
    return forward.transpose(3, 4, 5, 0, 1, 2).reshape(128, 128)


def twist_table():
    angle = 2 * np.pi * np.outer(np.arange(ROWS), np.arange(DEV)) / NX
    return np.concatenate([np.cos(angle), np.sin(angle)]).astype(np.float32)


def turn_table():
    angle = 2 * np.pi * np.outer(np.arange(MODES), np.arange(DEV)) / NZ
    table = np.stack([np.cos(angle), np.sin(angle)]) / math.sqrt(NZ)
    return table.reshape(2 * MODES, DEV).astype(np.float32)


def matrix_tables():
    dft = dft_table().reshape(4 * DEV, DEV)
    sides = [split_table(t) for t in (inner_table(-1.0), inverse_inner())]
    return np.concatenate([dft] + [np.concatenate([t[0], t[1]], 1) for t in sides], 0)


def angle_tables():
    return np.concatenate([twist_table(), turn_table()], 0)


def dot3(left, right):
    lh, ll = left
    rh, rl = right
    out = jnp.dot(lh, rh, preferred_element_type=F32)
    out += jnp.dot(ll, rh, preferred_element_type=F32)
    out += jnp.dot(lh, rl, preferred_element_type=F32)
    return out


def long_dft(blocks, mats, sign):
    rows = []
    for real, imag in blocks:
        if sign < 0:
            rows.append(jnp.concatenate([real, imag], 1))
            rows.append(jnp.concatenate([imag, -real], 1))
        else:
            rows.append(jnp.concatenate([real, -imag], 1))
            rows.append(jnp.concatenate([imag, real], 1))
    table = (mats[: 2 * DEV, :], mats[2 * DEV : 4 * DEV, :])
    out = dot3(split(jnp.concatenate(rows, 0)), table)
    return [
        (out[128 * c : 128 * c + 64], out[128 * c + 64 : 128 * c + 128])
        for c in range(len(blocks))
    ]


def read_lines(ref, which, count):
    blocks = []
    for c in which:
        lines = ref[pl.ds(c, DEV, stride=count), :].T
        blocks.append((lines[:64], lines[64:]))
    return blocks


def write_lines(ref, blocks):
    for c, (real, imag) in enumerate(blocks):
        ref[pl.ds(c, DEV, stride=len(blocks)), :] = jnp.concatenate([real, imag], 0).T


def position():
    return lax.axis_index("strike") * 4 + lax.axis_index("dip")


def send_half(ref, field, angles, mats):
    halves = ([], [])
    lasts = []
    lane = lax.broadcasted_iota(jnp.int32, (16, DEV), 1)
    sign = 1.0 - 2.0 * (lane & 1).astype(F32)
    for real, imag in dip_forward(field, angles):
        lasts.append(jnp.sum(real[:16] * sign, 1, keepdims=True))
        for rows, at in zip(halves, (0, 16)):
            re, im = real[at : at + 32], imag[at : at + 32]
            rows.append(jnp.concatenate([re, im], 1))
            rows.append(jnp.concatenate([im, -re], 1))
    outs = []
    for rows, lanes in zip(halves, (slice(0, 128), slice(128, 256))):
        table = (mats[: 2 * DEV, lanes], mats[2 * DEV : 4 * DEV, lanes])
        outs.append(dot3(split(jnp.concatenate(rows, 0)), table))
    out = jnp.concatenate(outs, 1)
    pieces = []
    for c, last in enumerate(lasts):
        pieces.append(out[64 * c : 64 * c + 32])
        pieces.append(jnp.where(lane == 0, last, out[64 * c + 32 : 64 * c + 48]))
        pieces.append(out[64 * c + 48 : 64 * c + 64])
    ref[...] = jnp.concatenate(pieces, 0).T


def receive_half(ref):
    device = position()
    low = jnp.where(device < DEV // 2, 1.0, 0.0)
    zero = jnp.where(device == 0, 1.0, 0.0)
    up = 1.0 - low
    lines = ref[...].T
    blocks = []
    for c in range(2):
        line = lines[64 * c : 64 * c + 64]
        ar, br, ai, bi = [line[16 * i : 16 * i + 16] for i in range(4)]
        none = jnp.zeros_like(ar)
        real = [low * ar, low * br + up * ar, up * br + zero * ai, none]
        imag = [(low - zero) * ai, low * bi + up * ai, up * bi, none]
        blocks.append((jnp.concatenate(real, 0), jnp.concatenate(imag, 0)))
    return blocks


def turns(angles):
    cos = [angles[32 + m : 33 + m, :] for m in range(4)]
    sin = [angles[36 + m : 37 + m, :] for m in range(4)]
    return cos, sin


def dip_forward(field, angles):
    cos, sin = turns(angles)
    blocks = []
    for x0, x1, x2, x3 in field:
        even, odd, f, g = x0 + x2, x1 + x3, x0 - x2, x1 - x3
        y0, y2 = even + odd, even - odd
        real = [y0 * cos[0], f * cos[1] - g * sin[1], y2 * cos[2], f * cos[3] + g * sin[3]]
        imag = [
            jnp.zeros_like(y0),
            -(f * sin[1] + g * cos[1]),
            -(y2 * sin[2]),
            g * cos[3] - f * sin[3],
        ]
        blocks.append((jnp.concatenate(real, 0), jnp.concatenate(imag, 0)))
    return blocks


def dip_inverse(lines, angles, mats, packed):
    cos, sin = turns(angles)
    lane = lax.broadcasted_iota(jnp.int32, (16, DEV), 1)
    sign = (1.0 - 2.0 * (lane & 1).astype(F32)) * (1.0 / math.sqrt(NZ))
    lasts = [imag[:16, :1] for _, imag in lines]
    field = []
    for (real, imag), last in zip(long_dft(lines, mats, 1), lasts):
        re = [real[16 * m : 16 * m + 16] for m in range(4)]
        im = [imag[16 * m : 16 * m + 16] for m in range(4)]
        u = [cos[m] * re[m] - sin[m] * im[m] for m in range(4)]
        v1 = cos[1] * im[1] + sin[1] * re[1]
        v3 = cos[3] * im[3] + sin[3] * re[3]
        a, b, c, d = u[0] + u[2], u[0] - u[2], u[1] + u[3], v3 - v1
        if packed:
            a, b = a + sign * last, b + sign * last
        field.append(jnp.concatenate([a + c, b + d, a - c, b - d], 0))
    return field


def friction(force, prestress, strength, state):
    load_strike = prestress[0] + force[0]
    load_dip = prestress[1] + force[1]
    traction = jnp.sqrt(load_strike * load_strike + load_dip * load_dip)
    factor = jnp.exp(-state)
    ratio = traction / factor
    estimate = jnp.minimum(traction / strength, jnp.log(ratio + jnp.sqrt(ratio * ratio + 1.0)))
    half = 0.5 * factor
    for _ in range(NEWTON):
        up, down = jnp.exp(estimate), jnp.exp(-estimate)
        residual = traction - strength * estimate - half * (up - down)
        estimate = estimate + residual / (strength + half * (up + down))
    slip_speed = 2.0 * (traction - strength * estimate)
    scale = slip_speed / jnp.maximum(traction, 1.0)
    rates = [scale * load_strike, scale * load_dip]
    return rates, state + 0.5 * (factor - 0.5 * slip_speed)


def pack_rest_kernel(prestress, normal, effect, state, *outs):
    own = lax.axis_index("dip")
    for i, out in enumerate(outs):
        rows = pl.ds(pl.multiple_of(lax.rem(own + i, 4) * 16, 16), 16)
        for c in range(2):
            out[16 * c : 16 * c + 16, :] = prestress[c, rows, :]
        out[32:48, :] = normal[rows, :] * effect[rows, :]
        out[48:64, :] = state[rows, :]


def first_kernel(fields, angles, mats, out):
    field = [[fields[d, 16 * c : 16 * c + 16, :] for d in range(4)] for c in range(3)]
    write_lines(out, long_dft(dip_forward(field, angles), mats, -1))


def middle_kernel(lines, part0, part1, part2, part3, angles, mats, out, state_out, fields, opening):
    own = lax.axis_index("dip")
    for i, part in enumerate((part0, part1, part2, part3)):
        rows = pl.ds(pl.multiple_of(lax.rem(own + 4 - i, 4) * 16, 16), 16)
        for c in range(3):
            fields[c, rows, :] = part[16 * c : 16 * c + 16, :]
        state_out[rows, :] = part[48:64, :]
    force = dip_inverse(read_lines(lines, (0, 1, 2), 3), angles, mats, False)
    opening[...] = 2.0 * force[2]
    rates, state = friction(force, (fields[0], fields[1]), fields[2], state_out[...])
    state_out[...] = state
    field = [[r[16 * d : 16 * d + 16] for d in range(4)] for r in rates]
    send_half(out, field, angles, mats)


def last_kernel(lines, fields, state_in, opening, angles, mats, out):
    force = dip_inverse(read_lines(lines, (0, 1), 2), angles, mats, True)
    rates, state = friction(force, (fields[0], fields[1]), fields[2], state_in[...])
    for d in range(4):
        for c, value in enumerate(rates + [opening, state]):
            out[d, 16 * c : 16 * c + 16, :] = value[16 * d : 16 * d + 16, :]


def unpack_kernel(gathered, rates, state):
    for d in range(4):
        rows = slice(16 * d, 16 * d + 16)
        for c in range(3):
            rates[c, rows, :] = gathered[d, 16 * c : 16 * c + 16, :]
        state[rows, :] = gathered[d, 48:64, :]


def mixing(kz, kx, lags):
    shape = kz.shape
    mz = jnp.where(2 * kz < NZ, kz, kz - NZ)
    mx = jnp.where(2 * kx < NX, kx, kx - NX)
    qz = mz.astype(F32) * (2.0 * math.pi / NZ)
    qx = mx.astype(F32) * (2.0 * math.pi / NX)
    q = jnp.sqrt(qx * qx + qz * qz)
    anchor = (mz == 0) & (mx == 0)
    safe = jnp.where(anchor, 1.0, q)
    ex = jnp.where(anchor, 1.0, qx / safe)
    ez = jnp.where(anchor, 0.0, qz / safe)
    xx, xz, zz = ex * ex, ex * ez, ez * ez
    decay = jnp.exp(-0.025 * q)
    envelope = -0.25 * q
    first = [jnp.cos(0.5 * s * q) for s in (1.0, 0.6, 1.7)]
    before = [jnp.ones(shape, F32)] * 3
    now = first
    out = []
    for _ in range(lags):
        envelope = envelope * decay
        two, three, one = [envelope * c for c in now]
        out.append((xx * two + zz * three, xz * (two - three), zz * two + xx * three, one))
        now, before = [2.0 * f * c - p for f, c, p in zip(first, now, before)], now
    return out


def history_kernel(history, lengths, past1, past2, coef, held, reach):
    device = position()
    for k1 in range(16):
        lanes = slice(DEV * k1, DEV * k1 + DEV)
        rows = slice(4 * k1, 4 * k1 + 4)
        reach[rows, :] = lengths[:, lanes].astype(F32)
    for lag in range(3):
        for c in range(3):
            for part in range(2):
                line = history[lag, c, part].astype(F32)
                for k1 in range(16):
                    held[lag, c, part, 4 * k1 : 4 * k1 + 4, :] = line[:, DEV * k1 : DEV * k1 + DEV]
    shape = (64, DEV)
    row = lax.broadcasted_iota(jnp.int32, shape, 0)
    kx = (row >> 2) * DEV + lax.broadcasted_iota(jnp.int32, shape, 1)
    m = row & 3
    mix = mixing(device * MODES + m, kx, 4)
    origin = jnp.where(device == 0, 0, 64)
    guest = (m + origin) == 2
    upper = jnp.where(device < DEV // 2, 0, 1)
    weight = jnp.where((m == upper) | (m == upper + 1), 2.0, 0.0)
    weight = jnp.where(guest | ((m + origin) == 0), 1.0, weight)
    cross = jnp.where((kx == NX // 2) & (weight == 2.0), 0.0, weight)
    new = mixing(jnp.where(guest, NZ // 2, device * MODES + m), kx, 1)[0]
    coef[7] = weight * new[0]
    coef[8] = cross * new[1]
    coef[9] = weight * new[2]
    coef[10] = jnp.where(guest, 1.0, 0.0)
    length = reach[...]
    masked = [None] + [
        [jnp.where(length > float(lag), m, 0.0) for m in mix[lag]] for lag in range(1, 4)
    ]
    twice = 2.0 * mix[0][3]
    for i in range(3):
        coef[i] = mix[0][i]
        coef[4 + i] = masked[1][i]
    coef[3] = twice * mix[0][3] + masked[1][3]
    for part in range(2):
        rows = slice(64 * part, 64 * part + 64)
        totals = []
        for skip in (1, 2):
            total = [0.0, 0.0, 0.0]
            for lag in range(skip, 4):
                ss, sd, dd, op = masked[lag]
                a, b, c = [held[lag - skip, i, part] for i in range(3)]
                total[0] = total[0] + (ss * a + sd * b)
                total[1] = total[1] + (sd * a + dd * b)
                total[2] = total[2] + op * c
            totals.append(total)
        for i in range(2):
            past1[i, rows, :] = totals[0][i]
            past2[i, rows, :] = totals[1][i]
        past1[2, rows, :] = twice * totals[0][2] + totals[1][2]


def spectrum_of(blocks, angles, mats):
    blocks = long_dft(blocks, mats, -1)
    cos = jnp.concatenate([angles[0:16, :]] * 4, 0)
    sin = jnp.concatenate([angles[16:32, :]] * 4, 0)
    turned = [
        jnp.concatenate([re * cos + im * sin, im * cos - re * sin], 0) for re, im in blocks
    ]
    inner = (mats[1024:1152, :128], mats[1024:1152, 128:])
    return dot3(inner, split(jnp.concatenate(turned, 1)))


def back_to_rows(force, angles, mats):
    back = (mats[1152:1280, :128], mats[1152:1280, 128:])
    blocks = dot3(back, split(jnp.concatenate(force, 1)))
    cos = jnp.concatenate([angles[0:16, :]] * 4, 0)
    sin = jnp.concatenate([angles[16:32, :]] * 4, 0)
    turned = []
    for c in range(len(force)):
        re, im = blocks[:64, DEV * c : DEV * c + DEV], blocks[64:, DEV * c : DEV * c + DEV]
        turned.append((re * cos - im * sin, im * cos + re * sin))
    return long_dft(turned, mats, 1)


def both_parts(coef, i):
    return jnp.concatenate([coef[i]] * 2, 0)


def apply_mix(coef, at, spec):
    ss, sd, dd = [both_parts(coef, at + i) for i in range(3)]
    s, d = spec[:, :DEV], spec[:, DEV : 2 * DEV]
    return [ss * s + sd * d, sd * s + dd * d]


def mode_kernel_first(lines, past, past_next, coef, angles, mats, out, older):
    spec = spectrum_of(read_lines(lines, (0, 1, 2), 3), angles, mats)
    for c, f in enumerate(apply_mix(coef, 4, spec)):
        older[c] = f + past_next[c]
    force = apply_mix(coef, 0, spec) + [both_parts(coef, 3) * spec[:, 2 * DEV :]]
    force = [f + past[c] for c, f in enumerate(force)]
    write_lines(out, back_to_rows(force, angles, mats))


def mode_kernel_second(lines, older, coef, angles, mats, out):
    spec = spectrum_of(receive_half(lines), angles, mats)
    guest = both_parts(coef, 10)
    force = apply_mix(coef, 7, spec)
    guests = [guest * f for f in force]
    force = [f - g + older[c] for c, (f, g) in enumerate(zip(force, guests))]
    extra = guests[0] + pltpu.roll(guests[1], 1, 0)
    strike, dip, (alone, _) = back_to_rows(force + [extra], angles, mats)
    zero = jnp.where(position() == 0, 1.0, 0.0)
    blocks = []
    for (real, imag), at in ((strike, 32), (dip, 48)):
        head = (1.0 - zero) * imag[:16] + zero * alone[at : at + 16]
        blocks.append((real, jnp.concatenate([head, imag[16:]], 0)))
    write_lines(out, blocks)


def call(kernel, outs, *args, scratch=(), grant=20, work=2.0):
    return pl.pallas_call(
        kernel,
        out_shape=[jax.ShapeDtypeStruct(s, F32) for s in outs],
        scratch_shapes=scratch,
        compiler_params=pltpu.CompilerParams(vmem_limit_bytes=grant << 20),
        cost_estimate=pl.CostEstimate(
            flops=int(work * 1e9), bytes_accessed=int(work * 3e6), transcendentals=0
        ),
    )(*args)


def exchange(lines):
    lanes = lines.shape[0] // DEV * 128
    swapped = lax.all_to_all(lines.reshape(DEV, 1, lanes), BOTH, 0, 0, tiled=True)
    return swapped.reshape(lines.shape)


def shards(slip_rate, history, lengths, prestress, normal_stress, direct_effect, state_log):
    mats, angles = matrix_tables(), angle_tables()
    three, two, one = (3 * DEV, 128), (2 * DEV, 128), (DEV, 128)
    packed = slip_rate.reshape(3, 4, 16, 256).transpose(1, 0, 2, 3).reshape(4, 48, 256)
    slip = lax.all_to_all(packed, "dip", 0, 0, tiled=True)
    (out,) = call(first_kernel, [three], slip, angles, mats)
    lines = exchange(out)
    parts = call(
        pack_rest_kernel,
        [(64, 256)] * 4,
        prestress,
        normal_stress,
        direct_effect,
        state_log,
    )
    parts = [
        lax.ppermute(part, "dip", [(j, (j + i) % 4) for j in range(4)]) if i else part
        for i, part in enumerate(parts)
    ]
    past1, past2, coef = call(
        history_kernel,
        [(3, 128, 256), (2, 128, 256), (11, 64, 256)],
        history,
        lengths,
        scratch=[pltpu.VMEM((3, 3, 2, 64, 256), F32), pltpu.VMEM((64, 256), F32)],
    )
    lines, parts, past1, past2, coef = lax.optimization_barrier(
        (lines, parts, past1, past2, coef)
    )
    out, older = call(
        mode_kernel_first, [three, (2, 128, 256)], lines, past1, past2, coef, angles, mats
    )
    out, state, fields, opening = call(
        middle_kernel,
        [one, (64, 256), (3, 64, 256), (64, 256)],
        exchange(out),
        *parts,
        angles,
        mats,
    )
    (out,) = call(mode_kernel_second, [two], exchange(out), older, coef, angles, mats)
    (out,) = call(
        last_kernel, [(4, 64, 256)], exchange(out), fields, state, opening, angles, mats
    )
    gathered = lax.all_to_all(out, "dip", 0, 0, tiled=True)
    rates, state = call(unpack_kernel, [(3, 64, 256), (64, 256)], gathered)
    return rates, state


def solution(mesh):
    return jax.shard_map(
        shards,
        mesh=mesh,
        in_specs=(
            P(None, "strike", "dip"),
            P(None, None, None, ("strike", "dip"), None),
            P(("strike", "dip"), None),
            P(None, "strike", "dip"),
            P("strike", "dip"),
            P("strike", "dip"),
            P("strike", "dip"),
        ),
        out_specs=(P(None, "strike", "dip"), P("strike", "dip")),
        check_vma=False,
    )
```
